32 devices in a mesh: gx: 8 (over z, x), row: 4 (over y, core).
Axes of the slice: x: 2, y: 2, z: 4, core: 2. Of those that a mesh axis runs over, the one named last changes fastest.
Arguments:
- adjoint_vectors: float32 [2, 5, 32, 192, 128], P(None, None, 'gx', 'row'), may hold values from -6 to 6
- base_density: float32 [32, 192, 128], P('gx', 'row'), may hold values from 0.6 to 1.4
- base_velocity: float32 [3, 32, 192, 128], P(None, 'gx', 'row'), may hold values from -3 to 3
- base_pressure: float32 [32, 192, 128], P('gx', 'row'), may hold values from 0.5 to 1.5
Outputs:
- adjoint_out: float32 [2, 5, 32, 192, 128], P(None, None, 'gx', 'row')
The draws below stay inside these ranges and needn't reach their ends.
All inputs are finite; a program needn't handle non-finite values.
Results may differ from the reference program's by a relative error of at most 0.0003.
Values sent between devices are 32-bit elements; how exact they have to be, the bound alone decides.
No kernel may reach another device: no remote copies, remote signals or barrier semaphores. Data moves between devices by JAX's collectives and lax.ppermute only.
A program may use at most 64 MiB of HBM per device.

```python
import jax
import jax.numpy as jnp
from jax import lax

NTH = 128
NV = 2
NX = 32
NR = 192


def shard_levels(rng, shape, shards, smallest, high):
    def one(dim, blocks):
        draws = jax.random.uniform(jax.random.fold_in(jax.random.fold_in(rng, 6), dim), (blocks,), jnp.float32, smallest / len(shards), high / len(shards))
        return jnp.repeat(jnp.exp(draws), shape[dim] // blocks).reshape((-1,) + (1,) * (len(shape) - dim - 1))

    level = one(*shards[0])
    for cut in shards[1:]:
        level = level * one(*cut)
    return level


def scatter_about(key, dims, width, limit, cuts=(), held_as=jnp.bfloat16):
    result = width * jax.random.normal(key, dims, jnp.float32)
    if cuts:
        result = result * shard_levels(key, dims, cuts, -0.22, 0.18)
    return jnp.clip(result, -limit, limit).astype(held_as)


def setup_inputs(seed: int = 0) -> dict:
    seeds = jax.random.split(jax.random.key(seed), 5)
    return {
        "adjoint_vectors": scatter_about(seeds[0], (NV, 5, NX, NR, NTH), 1.0, 6.0, ((2, 8), (3, 4)), jnp.float32),
        "base_density": jnp.clip(0.6 + 0.79999995 * jax.random.uniform(seeds[1], (NX, NR, NTH), jnp.float32) ** shard_levels(seeds[1], (NX, NR, NTH), ((0, 8), (1, 4)), -0.2, 0.2), 0.6, 1.4),
        "base_velocity": scatter_about(seeds[2], (3, NX, NR, NTH), 0.6, 3.0, ((1, 8), (2, 4)), jnp.float32),
        "base_pressure": jnp.clip(0.5 + 1.0 * jax.random.uniform(seeds[3], (NX, NR, NTH), jnp.float32) ** shard_levels(seeds[3], (NX, NR, NTH), ((0, 8), (1, 4)), -0.2, 0.2), 0.5, 1.5),
    }


gamma_ratio = 1.4
viscosity = 0.1
time_step = 0.3


def theta_tables(azimuth):
    spacing = 2.0 * jnp.pi / azimuth
    index = jnp.arange(azimuth, dtype=jnp.int32)
    offset = index[:, None] - index[None, :]
    parity = jnp.mod(offset, 2).astype(jnp.float32)
    signs = 1.0 - 2.0 * parity
    angle = offset.astype(jnp.float32) * (spacing / 2.0)
    diagonal = offset == 0
    tangent = jnp.where(diagonal, 1.0, jnp.tan(angle))
    sine = jnp.where(diagonal, 1.0, jnp.sin(angle))
    first_table = jnp.where(diagonal, 0.0, 0.5 * signs * spacing / tangent).astype(jnp.float32)
    second_table = jnp.where(diagonal, -jnp.pi ** 2 / 3.0 - spacing ** 2 / 6.0, -0.5 * signs * spacing ** 2 / (sine * sine)).astype(jnp.float32)
    return first_table, second_table


def radial_factor(rows, total_rows):
    return (1.0 / (1.0 + (rows.astype(jnp.float32) + 0.5) / total_rows))[:, None]


def shifted(padded, start, axis):
    axis = padded.ndim + axis
    length = padded.shape[axis] - 4
    return lax.slice_in_dim(padded, start, start + length, axis=axis)


def first_diff(padded, axis):
    return (8.0 * (shifted(padded, 3, axis) - shifted(padded, 1, axis)) - (shifted(padded, 4, axis) - shifted(padded, 0, axis))) / 12.0


def second_diff(padded, axis):
    return (-shifted(padded, 4, axis) + 16.0 * shifted(padded, 3, axis) - 30.0 * shifted(padded, 2, axis) + 16.0 * shifted(padded, 1, axis) - shifted(padded, 0, axis)) / 12.0


def azimuthal(field, table):
    shape = field.shape
    flat = field.reshape(-1, shape[-1])
    return jnp.dot(flat, table.T, precision=lax.Precision.HIGHEST).reshape(shape)


def flux(fields, base, direction):
    comp = 1 + direction
    density = base[0]
    safe_density = jnp.where(density > 0.0, density, 1.0)
    speed = base[comp]
    pressure = base[4]
    parts = []
    for member in range(5):
        value = fields[..., member, :, :, :]
        if member == 0:
            parts.append(speed * value)
        elif member == comp:
            parts.append(density * fields[..., 0, :, :, :] + speed * value + gamma_ratio * pressure * fields[..., 4, :, :, :])
        elif member == 4:
            parts.append(fields[..., comp, :, :, :] / safe_density + speed * value)
        else:
            parts.append(speed * value)
    return jnp.stack(parts, axis=-4)


def combine(flux_x, flux_r, fields_x, fields_r, flux_theta, core, first_table, second_table, factor):
    advect = first_diff(flux_x, -3) + first_diff(flux_r, -2) + factor * azimuthal(flux_theta, first_table)
    diffuse = second_diff(fields_x, -3) + second_diff(fields_r, -2) + azimuthal(core, second_table)
    return advect + viscosity * diffuse


def adjoint_rhs(fields, base, first_table, second_table, factor):
    pad_x = lambda arr: jnp.pad(arr, ((0, 0), (2, 2), (0, 0), (0, 0)))
    pad_r = lambda arr: jnp.pad(arr, ((0, 0), (0, 0), (2, 2), (0, 0)))
    flux_x = pad_x(flux(fields, base, 0))
    flux_r = pad_r(flux(fields, base, 1))
    flux_theta = flux(fields, base, 2)
    return combine(flux_x, flux_r, pad_x(fields), pad_r(fields), flux_theta, fields, first_table, second_table, factor)


def reference(adjoint_vectors, base_density, base_velocity, base_pressure):
    base = jnp.concatenate([base_density[None], base_velocity, base_pressure[None]], axis=0)
    first_table, second_table = theta_tables(adjoint_vectors.shape[-1])
    total_rows = adjoint_vectors.shape[3]
    factor = radial_factor(jnp.arange(total_rows, dtype=jnp.int32), total_rows)
    results = []
    for vector in range(adjoint_vectors.shape[0]):
        start = adjoint_vectors[vector]
        section_one = start + 0.5 * time_step * adjoint_rhs(start, base, first_table, second_table, factor)
        results.append(start + time_step * adjoint_rhs(section_one, base, first_table, second_table, factor))
    return jnp.stack(results, axis=0)
```

```python
import functools

import jax
import jax.numpy as jnp
import ml_dtypes
import numpy as np
from jax import lax
from jax.experimental import pallas as pl
from jax.experimental.pallas import tpu as pltpu
from jax.sharding import PartitionSpec as P

gamma_ratio = 1.4
viscosity = 0.1
time_step = 0.3

A1 = 8.0 / 12.0
A2 = 1.0 / 12.0
B1 = viscosity * 16.0 / 12.0
B2 = viscosity / 12.0
CENTRE = -2.0 * viscosity * 30.0 / 12.0
PAD = 8


def theta_table(azimuth):
    spacing = 2.0 * np.pi / azimuth
    index = np.arange(azimuth)
    offset = index[:, None] - index[None, :]
    signs = np.where(offset % 2 == 0, 1.0, -1.0)
    angle = offset * (spacing / 2.0)
    diagonal = offset == 0
    tangent = np.where(diagonal, 1.0, np.tan(angle))
    sine = np.where(diagonal, 1.0, np.sin(angle))
    first = np.where(diagonal, 0.0, 0.5 * signs * spacing / tangent)
    second = np.where(
        diagonal, -(np.pi**2) / 3.0 - spacing**2 / 6.0, -0.5 * signs * spacing**2 / (sine * sine)
    )
    table = np.concatenate([first.T, viscosity * second.T], axis=0).astype(np.float32)
    high = table.astype(ml_dtypes.bfloat16)
    low = (table - high.astype(np.float32)).astype(ml_dtypes.bfloat16)
    return np.concatenate([high, low], axis=1)


def section(
    dt, get, start, rho_ref, vel_ref, pr_ref, fac_ref, tab_ref,
    out_ref, xlo_ref, xhi_ref, rlo_ref, rhi_ref,
    wp, fr, fx, xh, xl, ys,
):
    cells, rows, width = rho_ref.shape
    step = 16
    zeros = jnp.zeros((PAD, width), jnp.float32)
    for f in range(5):
        for c in range(cells):
            for buf in (wp, fr):
                buf[f, c, 0:PAD] = zeros
                buf[f, c, PAD + rows : 2 * PAD + rows] = zeros
    for c in range(cells):
        for r in range(0, rows, step):
            at = slice(r, r + step)
            rho = rho_ref[c, at]
            inv = 1.0 / rho
            pg = gamma_ratio * pr_ref[c, at]
            fac = fac_ref[at]
            w = [get(f, c, r, step) for f in range(5)]
            q = rho * w[0] + pg * w[4]
            for d in range(3):
                speed = vel_ref[d, c, at]
                for f in range(5):
                    flow = speed * w[f]
                    if f == 1 + d:
                        flow = flow + q
                    elif f == 4:
                        flow = flow + w[1 + d] * inv
                    if d == 0:
                        fx[f, c, at] = flow
                    elif d == 1:
                        fr[f, c, PAD + r : PAD + r + step] = flow
                    else:
                        flow = flow * fac
                        high = flow.astype(jnp.bfloat16)
                        k = (f * cells + c) * rows + r
                        xh[k : k + step, 0:width] = high
                        xl[k : k + step, 0:width] = (flow - high.astype(jnp.float32)).astype(jnp.bfloat16)
            for f in range(5):
                wp[f, c, PAD + r : PAD + r + step] = w[f]
                high = w[f].astype(jnp.bfloat16)
                k = (f * cells + c) * rows + r
                xh[k : k + step, width : 2 * width] = high
                xl[k : k + step, width : 2 * width] = (w[f] - high.astype(jnp.float32)).astype(jnp.bfloat16)

    def radial(f, c, r, n):
        base = PAD + r
        sh = lambda buf, k: buf[f, c, base + k : base + k + n]
        return (
            A1 * (sh(fr, 1) - sh(fr, -1))
            - A2 * (sh(fr, 2) - sh(fr, -2))
            + B1 * (sh(wp, 1) + sh(wp, -1))
            - B2 * (sh(wp, 2) + sh(wp, -2))
        )

    for f in range(5):
        k = f * cells * rows
        span = cells * rows
        both = jnp.dot(xh[k : k + span], tab_ref[...], preferred_element_type=jnp.float32)
        low = jnp.dot(xl[k : k + span], tab_ref[:, 0:width], preferred_element_type=jnp.float32)
        ys[...] = (both[:, 0:width] + both[:, width:]) + low
        for r in range(0, rows, PAD):
            at = slice(r, r + PAD)
            ws = [wp[f, c, PAD + r : 2 * PAD + r] for c in range(cells)]
            fs = [fx[f, c, at] for c in range(cells)]

            def stream(i):
                total = None
                for k, a, b in ((1, A1, B1), (-1, -A1, B1), (2, -A2, -B2), (-2, A2, -B2)):
                    if 0 <= i + k < cells:
                        term = a * fs[i + k] + b * ws[i + k]
                        total = term if total is None else total + term
                return total

            xlo_ref[f, 0, at] = dt * stream(-2)
            xlo_ref[f, 1, at] = dt * stream(-1)
            xhi_ref[f, 0, at] = dt * stream(cells)
            xhi_ref[f, 1, at] = dt * stream(cells + 1)
            for c in range(cells):
                total = stream(c) + radial(f, c, r, PAD) + CENTRE * ws[c] + ys[c * rows + r : c * rows + r + PAD]
                out_ref[f, c, at] = start(f, c, r, PAD) + dt * total
        for c in range(cells):
            k = 2 * (f * cells + c)
            rlo_ref[k : k + 2] = dt * radial(f, c, -2, 2)
            rhi_ref[k : k + 2] = dt * radial(f, c, rows, 2)


def first_kernel(v, w_ref, rho_ref, vel_ref, pr_ref, fac_ref, tab_ref, *rest):
    get = lambda f, c, r, n: w_ref[v, f, c, r : r + n]
    section(0.5 * time_step, get, get, rho_ref, vel_ref, pr_ref, fac_ref, tab_ref, *rest)


def gather_edges(cells, rows, part_ref, left_ref, right_ref, rlo_ref, rhi_ref, write):
    for f in range(5):
        for c in range(cells):
            value = part_ref[f, c]
            if c < 2:
                value = value + left_ref[f, c]
            if c >= cells - 2:
                value = value + right_ref[f, c - (cells - 2)]
            write(f, c, value)
            k = 2 * (f * cells + c)
            yield f, c, k


def second_kernel(v, w_ref, part_ref, left_ref, right_ref, below_ref, above_ref,
                  rho_ref, vel_ref, pr_ref, fac_ref, tab_ref, *rest):
    *rest, s1 = rest
    cells, rows, width = rho_ref.shape

    def write(f, c, value):
        s1[f, c] = value

    for f, c, k in gather_edges(cells, rows, part_ref, left_ref, right_ref, below_ref, above_ref, write):
        s1[f, c, 0:2] += below_ref[k : k + 2]
        s1[f, c, rows - 2 : rows] += above_ref[k : k + 2]
    get = lambda f, c, r, n: s1[f, c, r : r + n]
    start = lambda f, c, r, n: w_ref[v, f, c, r : r + n]
    section(time_step, get, start, rho_ref, vel_ref, pr_ref, fac_ref, tab_ref, *rest)


def third_kernel(cells, rows, *refs):
    out_ref = refs[-1]
    for v in range(2):
        part_ref, left_ref, right_ref, below_ref, above_ref = refs[5 * v : 5 * v + 5]

        def write(f, c, value):
            out_ref[v, f, c] = value

        for f, c, k in gather_edges(cells, rows, part_ref, left_ref, right_ref, below_ref, above_ref, write):
            out_ref[v, f, c, 0:2] += below_ref[k : k + 2]
            out_ref[v, f, c, rows - 2 : rows] += above_ref[k : k + 2]


VM = pl.BlockSpec(memory_space=pltpu.VMEM)


def section_shapes(cells, rows, width):
    f32 = jnp.float32
    outs = [
        jax.ShapeDtypeStruct((5, cells, rows, width), f32),
        jax.ShapeDtypeStruct((5, 2, rows, width), f32),
        jax.ShapeDtypeStruct((5, 2, rows, width), f32),
        jax.ShapeDtypeStruct((5 * cells * 2, width), f32),
        jax.ShapeDtypeStruct((5 * cells * 2, width), f32),
    ]
    scratch = [
        pltpu.VMEM((5, cells, rows + 2 * PAD, width), f32),
        pltpu.VMEM((5, cells, rows + 2 * PAD, width), f32),
        pltpu.VMEM((5, cells, rows, width), f32),
        pltpu.VMEM((5 * cells * rows, 2 * width), jnp.bfloat16),
        pltpu.VMEM((5 * cells * rows, 2 * width), jnp.bfloat16),
        pltpu.VMEM((cells * rows, width), f32),
    ]
    return outs, scratch


PARAMS = pltpu.CompilerParams(vmem_limit_bytes=40 << 20)


def local(adjoint_vectors, base_density, base_velocity, base_pressure):
    _, _, cells, rows, width = adjoint_vectors.shape
    total_rows = lax.axis_size("row") * rows
    index = lax.axis_index("row") * rows + lax.broadcasted_iota(jnp.int32, (rows, width), 0)
    fac = 1.0 / (1.0 + (index.astype(jnp.float32) + 0.5) / total_rows)
    tab = jnp.asarray(theta_table(width))
    outs, scratch = section_shapes(cells, rows, width)
    steady = (base_density, base_velocity, base_pressure, fac, tab)

    gx, row = lax.axis_size("gx"), lax.axis_size("row")
    up = lambda n: [(i, i + 1) for i in range(n - 1)]
    down = lambda n: [(i + 1, i) for i in range(n - 1)]

    def trade(parts):
        part, xlo, xhi, rlo, rhi = parts
        left = lax.ppermute(xhi, "gx", up(gx))
        right = lax.ppermute(xlo, "gx", down(gx))
        below = lax.ppermute(rhi, "row", up(row))
        above = lax.ppermute(rlo, "row", down(row))
        return part, left, right, below, above

    def first(v):
        return pl.pallas_call(
            functools.partial(first_kernel, v), name=f"one_{v}", out_shape=outs, in_specs=[VM] * 6,
            out_specs=[VM] * 5, scratch_shapes=scratch, compiler_params=PARAMS,
        )(adjoint_vectors, *steady)

    def second(v, traded):
        return pl.pallas_call(
            functools.partial(second_kernel, v), name=f"two_{v}", out_shape=outs, in_specs=[VM] * 11,
            out_specs=[VM] * 5, scratch_shapes=scratch + [pltpu.VMEM((5, cells, rows, width), jnp.float32)],
            compiler_params=PARAMS,
        )(adjoint_vectors, *traded, *steady)

    traded = [trade(first(v)) for v in range(2)]
    traded = [trade(second(v, traded[v])) for v in range(2)]
    return pl.pallas_call(
        functools.partial(third_kernel, cells, rows), name="three",
        out_shape=jax.ShapeDtypeStruct(adjoint_vectors.shape, jnp.float32),
        in_specs=[VM] * 10, out_specs=VM, compiler_params=PARAMS,
    )(*traded[0], *traded[1])


def solution(mesh):
    in_specs = (
        P(None, None, "gx", "row", None),
        P("gx", "row", None),
        P(None, "gx", "row", None),
        P("gx", "row", None),
    )
    out_specs = P(None, None, "gx", "row", None)
    return jax.shard_map(local, mesh=mesh, in_specs=in_specs, out_specs=out_specs, check_vma=False)
```

```python
import functools

import jax
import jax.numpy as jnp
import ml_dtypes
import numpy as np
from jax import lax
from jax.experimental import pallas as pl
from jax.experimental.pallas import tpu as pltpu
from jax.sharding import PartitionSpec as P

gamma_ratio = 1.4
viscosity = 0.1
time_step = 0.3

A1 = 8.0 / 12.0
A2 = 1.0 / 12.0
B1 = viscosity * 16.0 / 12.0
B2 = viscosity / 12.0
CENTRE = -2.0 * viscosity * 30.0 / 12.0
PAD = 8


def theta_table(azimuth):
    spacing = 2.0 * np.pi / azimuth
    index = np.arange(azimuth)
    offset = index[:, None] - index[None, :]
    signs = np.where(offset % 2 == 0, 1.0, -1.0)
    angle = offset * (spacing / 2.0)
    diagonal = offset == 0
    tangent = np.where(diagonal, 1.0, np.tan(angle))
    sine = np.where(diagonal, 1.0, np.sin(angle))
    first = np.where(diagonal, 0.0, 0.5 * signs * spacing / tangent)
    second = np.where(
        diagonal, -(np.pi**2) / 3.0 - spacing**2 / 6.0, -0.5 * signs * spacing**2 / (sine * sine)
    )
    table = np.concatenate([first.T, viscosity * second.T], axis=0).astype(np.float32)
    high = table.astype(ml_dtypes.bfloat16)
    low = (table - high.astype(np.float32)).astype(ml_dtypes.bfloat16)
    return np.concatenate([high, low], axis=1)


def section(dt, parity, get, start, steady, out_ref, xp_ref, xd_ref, put_edges, wp, fr, fx, xh, xl, ys):
    rho_ref, vel_ref, inv_ref, pg_ref, fac_ref, tab_ref = steady
    cells, rows, width = rho_ref.shape
    step = 16
    zeros = jnp.zeros((PAD, width), jnp.float32)
    for f in range(5):
        for c in range(cells):
            for buf in (wp, fr):
                buf[f, c, 0:PAD] = zeros
                buf[f, c, PAD + rows : 2 * PAD + rows] = zeros
    for c in range(cells):
        for r in range(0, rows, step):
            at = slice(r, r + step)
            rho, inv, pg, fac = rho_ref[c, at], inv_ref[c, at], pg_ref[c, at], fac_ref[at]
            w = [get(f, c, r, step) for f in range(5)]
            q = rho * w[0] + pg * w[4]
            for d in range(3):
                speed = vel_ref[d, c, at]
                for f in range(5):
                    flow = speed * w[f]
                    if f == 1 + d:
                        flow = flow + q
                    elif f == 4:
                        flow = flow + w[1 + d] * inv
                    if d == 0:
                        fx[f, c, at] = flow
                    elif d == 1:
                        fr[f, c, PAD + r : PAD + r + step] = flow
                    else:
                        flow = flow * fac
                        high = flow.astype(jnp.bfloat16)
                        k = (f * cells + c) * rows + r
                        xh[k : k + step, 0:width] = high
                        xl[k : k + step, 0:width] = (flow - high.astype(jnp.float32)).astype(jnp.bfloat16)
            for f in range(5):
                wp[f, c, PAD + r : PAD + r + step] = w[f]
                high = w[f].astype(jnp.bfloat16)
                k = (f * cells + c) * rows + r
                xh[k : k + step, width : 2 * width] = high
                xl[k : k + step, width : 2 * width] = (w[f] - high.astype(jnp.float32)).astype(jnp.bfloat16)

    def radial(f, c, r, n):
        base = PAD + r
        sh = lambda buf, k: buf[f, c, base + k : base + k + n]
        return (
            A1 * (sh(fr, 1) - sh(fr, -1))
            - A2 * (sh(fr, 2) - sh(fr, -2))
            + B1 * (sh(wp, 1) + sh(wp, -1))
            - B2 * (sh(wp, 2) + sh(wp, -2))
        )

    for f in range(5):
        k = f * cells * rows
        span = cells * rows
        both = jnp.dot(xh[k : k + span], tab_ref[...], preferred_element_type=jnp.float32)
        low = jnp.dot(xl[k : k + span], tab_ref[:, 0:width], preferred_element_type=jnp.float32)
        ys[...] = (both[:, 0:width] + both[:, width:]) + low
        for r in range(0, rows, PAD):
            at = slice(r, r + PAD)
            ws = [wp[f, c, PAD + r : 2 * PAD + r] for c in range(cells)]
            fs = [fx[f, c, at] for c in range(cells)]

            def stream(i):
                total = None
                for k, a, b in ((1, A1, B1), (-1, -A1, B1), (2, -A2, -B2), (-2, A2, -B2)):
                    if 0 <= i + k < cells:
                        term = a * fs[i + k] + b * ws[i + k]
                        total = term if total is None else total + term
                return total

            for j in range(2):
                low_face = dt * stream(j - 2)
                high_face = dt * stream(cells + j)
                xp_ref[f, j, at] = jnp.where(parity == 0, high_face, low_face)
                xd_ref[f, j, at] = jnp.where(parity == 0, low_face, high_face)
            for c in range(cells):
                total = stream(c) + radial(f, c, r, PAD) + CENTRE * ws[c] + ys[c * rows + r : c * rows + r + PAD]
                out_ref[f, c, at] = start(f, c, r, PAD) + dt * total
        for c in range(cells):
            put_edges(f, c, dt * radial(f, c, -2, 2), dt * radial(f, c, rows, 2))


def edge_writer(v, cells, parity, rp_ref, rd_ref):
    def put(f, c, low_edge, high_edge):
        k = 2 * ((5 * v + f) * cells + c)
        rp_ref[k : k + 2] = jnp.where(parity == 0, high_edge, low_edge)
        rd_ref[k : k + 2] = jnp.where(parity == 0, low_edge, high_edge)

    return put


def first_kernel(half, total_rows, w_hbm, rho_hbm, vel_hbm, pr_hbm, tab_hbm,
                 part_ref, xp_ref, xd_ref, rp_ref, rd_ref,
                 w_ref, rho_ref, vel_ref, inv_ref, pg_ref, fac_ref, tab_ref,
                 wp, fr, fx, xh, xl, ys, sems):
    cells, rows, width = rho_ref.shape
    pairs = [
        (w_hbm.at[0], w_ref.at[0]), (rho_hbm, rho_ref), (pr_hbm, pg_ref), (vel_hbm, vel_ref),
        (tab_hbm, tab_ref), (w_hbm.at[1], w_ref.at[1]),
    ]
    copies = [pltpu.make_async_copy(a, b, sems.at[i]) for i, (a, b) in enumerate(pairs)]
    for copy in copies:
        copy.start()
    index = lax.axis_index("row") * rows + lax.broadcasted_iota(jnp.int32, (rows, width), 0)
    fac_ref[...] = 1.0 / (1.0 + (index.astype(jnp.float32) + 0.5) / total_rows)
    for copy in copies[:-1]:
        copy.wait()
    inv_ref[...] = 1.0 / rho_ref[...]
    pg_ref[...] = gamma_ratio * pg_ref[...]
    get = lambda f, c, r, n: w_ref[0, f, c, r : r + n]
    put = edge_writer(0, cells, lax.axis_index("row") % 2, rp_ref, rd_ref)
    steady = (rho_ref, vel_ref, inv_ref, pg_ref, fac_ref, tab_ref)
    section(0.5 * time_step, lax.axis_index("gx") % 2, get, get, steady, part_ref, xp_ref, xd_ref, put,
            wp, fr, fx, xh, xl, ys)
    copies[-1].wait()


def next_kernel(w_ref, rp0_ref, rd0_ref, rho_ref, vel_ref, inv_ref, pg_ref, fac_ref, tab_ref,
                part_ref, xp_ref, xd_ref, rp_ref, rd_ref, *scratch):
    cells, rows, width = rho_ref.shape
    half = 10 * cells
    rp_ref[0:half] = rp0_ref[...]
    rd_ref[0:half] = rd0_ref[...]
    get = lambda f, c, r, n: w_ref[1, f, c, r : r + n]
    put = edge_writer(1, cells, lax.axis_index("row") % 2, rp_ref, rd_ref)
    steady = (rho_ref, vel_ref, inv_ref, pg_ref, fac_ref, tab_ref)
    section(0.5 * time_step, lax.axis_index("gx") % 2, get, get, steady, part_ref, xp_ref, xd_ref, put, *scratch)


def add_faces(v, part_ref, xp_ref, xd_ref, rp_ref, rd_ref, out):
    _, cells, rows, _ = part_ref.shape
    column = lax.axis_index("gx") % 2
    line = lax.axis_index("row") % 2
    for f in range(5):
        for c in range(cells):
            out[f, c] = part_ref[f, c]
    for f in range(5):
        for j in range(2):
            out[f, (cells - 2) * (1 - column) + j] += xp_ref[f, j]
            out[f, (cells - 2) * column + j] += xd_ref[f, j]
    for f in range(5):
        for c in range(cells):
            k = 2 * ((5 * v + f) * cells + c)
            rp, rd = rp_ref[k : k + 2], rd_ref[k : k + 2]
            out[f, c, 0:2] += jnp.where(line == 0, rd, rp)
            out[f, c, rows - 2 : rows] += jnp.where(line == 0, rp, rd)


def second_kernel(v, *refs):
    w_ref, part_ref, xp_in, xd_in, rp_in, rd_in = refs[:6]
    refs = refs[6:]
    if v == 1:
        rp0_ref, rd0_ref, *refs = refs
    rho_ref, vel_ref, inv_ref, pg_ref, fac_ref, tab_ref, out_ref, xp_ref, xd_ref, rp_ref, rd_ref, *scratch, s1 = refs
    cells, rows, width = rho_ref.shape
    if v == 1:
        half = 10 * cells
        rp_ref[0:half] = rp0_ref[...]
        rd_ref[0:half] = rd0_ref[...]
    add_faces(v, part_ref, xp_in, xd_in, rp_in, rd_in, s1)
    get = lambda f, c, r, n: s1[f, c, r : r + n]
    start = lambda f, c, r, n: w_ref[v, f, c, r : r + n]
    put = edge_writer(v, cells, lax.axis_index("row") % 2, rp_ref, rd_ref)
    steady = (rho_ref, vel_ref, inv_ref, pg_ref, fac_ref, tab_ref)
    section(time_step, lax.axis_index("gx") % 2, get, start, steady, out_ref, xp_ref, xd_ref, put, *scratch)


def third_kernel(v, part_ref, xp_ref, xd_ref, rp_ref, rd_ref, *refs):
    out_hbm, value, sem = refs[-3:]
    add_faces(v, part_ref, xp_ref, xd_ref, rp_ref, rd_ref, value)
    copy = pltpu.make_async_copy(value, out_hbm.at[v], sem)
    copy.start()
    copy.wait()


VM = pl.BlockSpec(memory_space=pltpu.VMEM)
HB = pl.BlockSpec(memory_space=pltpu.HBM)
PARAMS = pltpu.CompilerParams(vmem_limit_bytes=40 << 20)


def local(adjoint_vectors, base_density, base_velocity, base_pressure):
    _, _, cells, rows, width = adjoint_vectors.shape
    f32 = jnp.float32
    shape = lambda *s: jax.ShapeDtypeStruct(s, f32)
    total_rows = lax.axis_size("row") * rows
    tab = jnp.asarray(theta_table(width))
    edge = 10 * cells
    part = [shape(5, cells, rows, width), shape(5, 2, rows, width), shape(5, 2, rows, width)]
    outs = lambda n: part + [shape(n * edge, width), shape(n * edge, width)]
    scratch = [
        pltpu.VMEM((5, cells, rows + 2 * PAD, width), f32),
        pltpu.VMEM((5, cells, rows + 2 * PAD, width), f32),
        pltpu.VMEM((5, cells, rows, width), f32),
        pltpu.VMEM((5 * cells * rows, 2 * width), jnp.bfloat16),
        pltpu.VMEM((5 * cells * rows, 2 * width), jnp.bfloat16),
        pltpu.VMEM((cells * rows, width), f32),
    ]

    def swap(value, axis, first):
        size = lax.axis_size(axis)
        pairs = [(i, i + 1) for i in range(0 if first else 1, size - 1, 2)]
        return lax.ppermute(value, axis, pairs + [(j, i) for i, j in pairs])

    *one, w, rho, vel, inv, pg, fac, table = pl.pallas_call(
        functools.partial(first_kernel, edge, total_rows), name="one_0",
        out_shape=outs(1) + [
            shape(2, 5, cells, rows, width), shape(cells, rows, width), shape(3, cells, rows, width),
            shape(cells, rows, width), shape(cells, rows, width), shape(rows, width),
            jax.ShapeDtypeStruct(tab.shape, tab.dtype),
        ],
        in_specs=[HB] * 5, out_specs=[VM] * 12, scratch_shapes=scratch + [pltpu.SemaphoreType.DMA((6,))],
        compiler_params=PARAMS,
    )(*(pltpu.with_memory_space_constraint(a, pltpu.HBM)
        for a in (adjoint_vectors, base_density, base_velocity, base_pressure, tab)))
    steady = (rho, vel, inv, pg, fac, table)
    parts = [None, None]
    parts[0], xp, xd, rp, rd = one
    faces = [(swap(xp, "gx", True), swap(xd, "gx", False)), None]
    parts[1], xp, xd, rp, rd = pl.pallas_call(
        next_kernel, name="one_1", out_shape=outs(2), in_specs=[VM] * 9, out_specs=[VM] * 5,
        scratch_shapes=scratch, compiler_params=PARAMS,
    )(w, rp, rd, *steady)
    faces[1] = (swap(xp, "gx", True), swap(xd, "gx", False))
    edges = (swap(rp, "row", True), swap(rd, "row", False))
    more = ()
    for v in range(2):
        parts[v], xp, xd, rp, rd = pl.pallas_call(
            functools.partial(second_kernel, v), name=f"two_{v}", out_shape=outs(1 + v),
            in_specs=[VM] * (12 + 2 * v), out_specs=[VM] * 5,
            scratch_shapes=scratch + [pltpu.VMEM((5, cells, rows, width), f32)], compiler_params=PARAMS,
        )(w, parts[v], *faces[v], *edges, *more, *steady)
        faces[v] = (swap(xp, "gx", True), swap(xd, "gx", False))
        more = (rp, rd)
    edges = (swap(rp, "row", True), swap(rd, "row", False))
    out = ()
    for v in range(2):
        out = (pl.pallas_call(
            functools.partial(third_kernel, v), name=f"three_{v}",
            out_shape=shape(*adjoint_vectors.shape), in_specs=[VM] * 5 + [HB] * v, out_specs=HB,
            scratch_shapes=[pltpu.VMEM((5, cells, rows, width), f32), pltpu.SemaphoreType.DMA],
            input_output_aliases={5: 0} if v else {}, compiler_params=PARAMS,
        )(parts[v], *faces[v], *edges, *out),)
    return out[0]


def solution(mesh):
    in_specs = (
        P(None, None, "gx", "row", None),
        P("gx", "row", None),
        P(None, "gx", "row", None),
        P("gx", "row", None),
    )
    out_specs = P(None, None, "gx", "row", None)
    return jax.shard_map(local, mesh=mesh, in_specs=in_specs, out_specs=out_specs, check_vma=False)
```

```python
import functools

import jax
import jax.numpy as jnp
import ml_dtypes
import numpy as np
from jax import lax
from jax.experimental import pallas as pl
from jax.experimental.pallas import tpu as pltpu
from jax.sharding import PartitionSpec as P

gamma_ratio = 1.4
viscosity = 0.1
time_step = 0.3

A1 = 8.0 / 12.0
A2 = 1.0 / 12.0
B1 = viscosity * 16.0 / 12.0
B2 = viscosity / 12.0
CENTRE = -2.0 * viscosity * 30.0 / 12.0
PAD = 8


def theta_table(azimuth):
    spacing = 2.0 * np.pi / azimuth
    index = np.arange(azimuth)
    offset = index[:, None] - index[None, :]
    signs = np.where(offset % 2 == 0, 1.0, -1.0)
    angle = offset * (spacing / 2.0)
    diagonal = offset == 0
    tangent = np.where(diagonal, 1.0, np.tan(angle))
    sine = np.where(diagonal, 1.0, np.sin(angle))
    first = np.where(diagonal, 0.0, 0.5 * signs * spacing / tangent)
    second = np.where(
        diagonal, -(np.pi**2) / 3.0 - spacing**2 / 6.0, -0.5 * signs * spacing**2 / (sine * sine)
    )
    table = np.concatenate([first.T, viscosity * second.T], axis=0).astype(np.float32)
    high = table.astype(ml_dtypes.bfloat16)
    low = (table - high.astype(np.float32)).astype(ml_dtypes.bfloat16)
    return np.concatenate([high, low], axis=1)


def fluxes(base_ref, c, at, w, directions):
    rho, pr = base_ref[0, c, at], base_ref[4, c, at]
    inv = 1.0 / rho
    pg = gamma_ratio * pr
    flows = []
    for v in range(2):
        q = rho * w[v][0] + pg * w[v][4]
        rows = []
        for d in directions:
            speed = base_ref[1 + d, c, at]
            flow = [speed * w[v][f] for f in range(5)]
            flow[1 + d] = flow[1 + d] + q
            flow[4] = flow[4] + w[v][1 + d] * inv
            rows.append(flow)
        flows.append(rows)
    return flows


def radial(fr, wp, v, f, c, r, n):
    base = PAD + r
    sh = lambda buf, k: buf[v, f, c, base + k : base + k + n]
    return (
        A1 * (sh(fr, 1) - sh(fr, -1))
        - A2 * (sh(fr, 2) - sh(fr, -2))
        + B1 * (sh(wp, 1) + sh(wp, -1))
        - B2 * (sh(wp, 2) + sh(wp, -2))
    )


def clear_pads(fr, wp):
    _, _, cells, padded, width = fr.shape
    zeros = jnp.zeros((PAD, width), jnp.float32)
    for v in range(2):
        for f in range(5):
            for c in range(cells):
                for buf in (wp, fr):
                    buf[v, f, c, 0:PAD] = zeros
                    buf[v, f, c, padded - PAD : padded] = zeros


def put_edges(dt, line, fr, wp, rp_ref, rd_ref):
    _, _, cells, padded, _ = fr.shape
    for v in range(2):
        for f in range(5):
            for c in range(cells):
                low = dt * radial(fr, wp, v, f, c, -2, 2)
                high = dt * radial(fr, wp, v, f, c, padded - 2 * PAD, 2)
                k = 2 * ((5 * v + f) * cells + c)
                rp_ref[k : k + 2] = jnp.where(line == 0, high, low)
                rd_ref[k : k + 2] = jnp.where(line == 0, low, high)


def section(dt, parity, line, half, get, start, base_ref, tab_ref, put, xp_ref, xd_ref, rp_ref, rd_ref,
            wp, fr, fx, xh, xl, ys):
    _, cells, rows, width = base_ref.shape
    total_rows = 2 * rows * lax.axis_size("row")
    row_start = lax.axis_index("row") * (2 * rows) + half * rows
    span = 2 * cells * rows
    clear_pads(fr, wp)

    def split(flow, k, lanes):
        both = jnp.concatenate(flow, axis=0)
        high = both.astype(jnp.bfloat16)
        xh[k : k + 2 * PAD, lanes] = high
        xl[k : k + 2 * PAD, lanes] = (both - high.astype(jnp.float32)).astype(jnp.bfloat16)

    for r in range(0, rows, PAD):
        at = slice(r, r + PAD)
        inside = slice(PAD + r, 2 * PAD + r)
        index = row_start + r + lax.broadcasted_iota(jnp.int32, (PAD, width), 0)
        fac = 1.0 / (1.0 + (index.astype(jnp.float32) + 0.5) / total_rows)
        for c in range(cells):
            w = [[get(v, f, c, r) for f in range(5)] for v in range(2)]
            flows = fluxes(base_ref, c, at, w, (0, 1, 2))
            for f in range(5):
                k = f * span + (c * (rows // PAD) + r // PAD) * 2 * PAD
                for v in range(2):
                    fx[v, f, c, at] = flows[v][0][f]
                    fr[v, f, c, inside] = flows[v][1][f]
                    wp[v, f, c, inside] = w[v][f]
                split([flows[v][2][f] * fac for v in range(2)], k, slice(0, width))
                split([w[v][f] for v in range(2)], k, slice(width, 2 * width))
    for f in range(5):
        both = jnp.dot(xh[f * span : (f + 1) * span], tab_ref[...], preferred_element_type=jnp.float32)
        low = jnp.dot(xl[f * span : (f + 1) * span], tab_ref[:, 0:width], preferred_element_type=jnp.float32)
        ys[...] = (both[:, 0:width] + both[:, width:]) + low
        for v in range(2):
            for r in range(0, rows, PAD):
                at = slice(r, r + PAD)
                ws = [wp[v, f, c, PAD + r : 2 * PAD + r] for c in range(cells)]
                fs = [fx[v, f, c, at] for c in range(cells)]

                def stream(i):
                    total = None
                    for k, a, b in ((1, A1, B1), (-1, -A1, B1), (2, -A2, -B2), (-2, A2, -B2)):
                        if 0 <= i + k < cells:
                            term = a * fs[i + k] + b * ws[i + k]
                            total = term if total is None else total + term
                    return total

                for j in range(2):
                    low_face = dt * stream(j - 2)
                    high_face = dt * stream(cells + j)
                    xp_ref[v, f, j, at] = jnp.where(parity == 0, high_face, low_face)
                    if xd_ref is not None:
                        xd_ref[v, f, j, at] = jnp.where(parity == 0, low_face, high_face)
                for c in range(cells):
                    k = (c * (rows // PAD) + r // PAD) * 2 * PAD + PAD * v
                    total = stream(c) + radial(fr, wp, v, f, c, r, PAD) + CENTRE * ws[c] + ys[k : k + PAD]
                    put(v, f, c, at, start(v, f, c, r) + dt * total)
    if rp_ref is not None:
        put_edges(dt, line, fr, wp, rp_ref, rd_ref)


def add_edges(line, rp_ref, rd_ref, out, cells):
    rows = out.shape[3]
    for v in range(2):
        for f in range(5):
            for c, place in cells:
                k = 2 * ((5 * v + f) * 4 + c)
                if not isinstance(c, int):
                    k = pl.multiple_of(k, 2)
                rp, rd = rp_ref[pl.ds(k, 2)], rd_ref[pl.ds(k, 2)]
                out[v, f, place, 0:2] += jnp.where(line == 0, rd, rp)
                out[v, f, place, rows - 2 : rows] += jnp.where(line == 0, rp, rd)


def add_faces(parity, xp_ref, xd_ref, out):
    cells = out.shape[2]
    for v in range(2):
        for f in range(5):
            for j in range(2):
                out[v, f, (cells - 2) * (1 - parity) + j] += xp_ref[v, f, j]
                out[v, f, (cells - 2) * parity + j] += xd_ref[v, f, j]


def all_cells(fn):
    for v in range(2):
        for f in range(5):
            for c in range(4):
                fn(v, f, c)


def place():
    column = lax.axis_index("gx") % 2
    return column, (column + lax.axis_index("row")) % 2


def load_kernel(w_hbm, rho_hbm, vel_hbm, pr_hbm, tab_hbm,
                own_ref, other_ref, outer_ref, inner_ref, base_ref, send_ref, tab_ref, sems):
    column, half = place()
    outer = 2 * column
    pairs = []
    for side, ref in ((1 - half, send_ref), (half, base_ref)):
        pairs.append((rho_hbm.at[:, side], ref.at[0]))
        pairs.append((vel_hbm.at[:, :, side], ref.at[1:4]))
        pairs.append((pr_hbm.at[:, side], ref.at[4]))
    pairs.append((w_hbm.at[:, :, pl.ds(outer, 2), 1 - half], outer_ref))
    pairs.append((w_hbm.at[:, :, pl.ds(2 - outer, 2), 1 - half], inner_ref))
    pairs.append((w_hbm.at[:, :, :, half], own_ref))
    pairs.append((w_hbm.at[:, :, :, 1 - half], other_ref))
    pairs.append((tab_hbm, tab_ref))
    copies = [pltpu.make_async_copy(a, b, sems.at[i]) for i, (a, b) in enumerate(pairs)]
    for copy in copies:
        copy.start()
    for copy in copies:
        copy.wait()


def own_first_kernel(own_ref, other_ref, base_ref, send_ref, tab_ref,
                     part_ref, xp_ref, xd_ref, rp_ref, rd_ref, rpo_ref, rdo_ref, wp, fr, *scratch):
    column, half = place()
    _, cells, rows, _ = base_ref.shape
    get = lambda v, f, c, r: own_ref[v, f, c, r : r + PAD]

    def put(v, f, c, at, value):
        part_ref[v, f, c, at] = value

    section(0.5 * time_step, column, half, half, get, get, base_ref, tab_ref, put,
            xp_ref, xd_ref, rp_ref, rd_ref, wp, fr, *scratch)
    for c in range(cells):
        for r in (0, rows - PAD):
            w = [[other_ref[v, f, c, r : r + PAD] for f in range(5)] for v in range(2)]
            flows = fluxes(send_ref, c, slice(r, r + PAD), w, (1,))
            for v in range(2):
                for f in range(5):
                    fr[v, f, c, PAD + r : 2 * PAD + r] = flows[v][0][f]
                    wp[v, f, c, PAD + r : 2 * PAD + r] = w[v][f]
    put_edges(0.5 * time_step, 1 - half, fr, wp, rpo_ref, rdo_ref)


def face_kernel(outer_ref, base_ref, xd_ref):
    column, _ = place()
    parity = 1 - column
    dt = 0.5 * time_step
    rows = outer_ref.shape[3]
    for r in range(0, rows, PAD):
        at = slice(r, r + PAD)
        w = [[[outer_ref[v, f, j, at] for f in range(5)] for v in range(2)] for j in range(2)]
        flows = [fluxes(base_ref, 2 * parity + j, at, w[j], (0,)) for j in range(2)]
        for v in range(2):
            for f in range(5):
                f0, f1 = flows[0][v][0][f], flows[1][v][0][f]
                w0, w1 = w[0][v][f], w[1][v][f]
                low = (-A2 * f0 - B2 * w0, (A1 * f0 + B1 * w0) + (-A2 * f1 - B2 * w1))
                high = ((-A1 * f1 + B1 * w1) + (A2 * f0 - B2 * w0), A2 * f1 - B2 * w1)
                for j in range(2):
                    xd_ref[v, f, j, at] = dt * jnp.where(parity == 0, low[j], high[j])


def partner_first_kernel(outer_ref, inner_ref, base_ref, tab_ref, w_ref, part_ref, xp_ref, *scratch):
    column, half = place()
    parity = 1 - column
    for v in range(2):
        for f in range(5):
            for j in range(2):
                w_ref[v, f, 2 * parity + j] = outer_ref[v, f, j]
                w_ref[v, f, 2 - 2 * parity + j] = inner_ref[v, f, j]
    get = lambda v, f, c, r: w_ref[v, f, c, r : r + PAD]

    def put(v, f, c, at, value):
        part_ref[v, f, c, at] = value

    section(0.5 * time_step, parity, half, half, get, get, base_ref, tab_ref, put,
            xp_ref, None, None, None, *scratch)


def second_kernel(own, *refs):
    w_ref, part_ref, xp_in, xd_in, rp_in, rd_in, base_ref, tab_ref = refs[:8]
    refs = refs[8:]
    column, half = place()
    parity = column if own else 1 - column
    if own:
        out_ref, xp_ref, xd_ref, rp_ref, rd_ref, *scratch, s1 = refs
        target = out_ref
    else:
        xp_own, inner_ref, outer_ref, xp_ref, xd_ref, rp_ref, rd_ref, *scratch, s1, target = refs

    def fill(v, f, c):
        s1[v, f, c] = part_ref[v, f, c]

    all_cells(fill)
    add_faces(parity, xp_in, xd_in, s1)
    add_edges(half, rp_in, rd_in, s1, [(c, c) for c in range(4)])
    get = lambda v, f, c, r: s1[v, f, c, r : r + PAD]
    start = lambda v, f, c, r: w_ref[v, f, c, r : r + PAD]

    def put(v, f, c, at, value):
        target[v, f, c, at] = value

    section(time_step, parity, half, half, get, start, base_ref, tab_ref, put,
            xp_ref, xd_ref, rp_ref, rd_ref, *scratch)
    if not own:
        for v in range(2):
            for f in range(5):
                for j in range(2):
                    inner_ref[v, f, j] = target[v, f, 2 - 2 * parity + j] + xp_own[v, f, j]
                    outer_ref[v, f, j] = target[v, f, 2 * parity + j]


def sum_kernel(a_ref, b_ref, out_ref):
    out_ref[...] = a_ref[...] + b_ref[...]


def own_last_kernel(part_ref, xp_ref, xd_ref, rp_ref, rd_ref, out_hbm, value, sem):
    column, half = place()

    def fill(v, f, c):
        value[v, f, c] = part_ref[v, f, c]

    all_cells(fill)
    add_faces(column, xp_ref, xd_ref, value)
    add_edges(half, rp_ref, rd_ref, value, [(c, c) for c in range(4)])
    copy = pltpu.make_async_copy(value, out_hbm.at[:, :, :, half], sem)
    copy.start()
    copy.wait()


def other_last_kernel(outer, back_ref, rp_ref, rd_ref, _, out_hbm, value, sem):
    column, half = place()
    first = 2 * column if outer else 2 - 2 * column
    value[...] = back_ref[...]
    add_edges(1 - half, rp_ref, rd_ref, value, [(first + j, j) for j in range(2)])
    copy = pltpu.make_async_copy(value, out_hbm.at[:, :, pl.ds(first, 2), 1 - half], sem)
    copy.start()
    copy.wait()


def second_kernel_par(*refs):
    refs = list(refs)
    xp_own2 = refs.pop(8)
    second_kernel(False, *refs[:8], xp_own2, *refs[8:])


VM = pl.BlockSpec(memory_space=pltpu.VMEM)
HB = pl.BlockSpec(memory_space=pltpu.HBM)
PARAMS = pltpu.CompilerParams(vmem_limit_bytes=40 << 20)


def local(adjoint_vectors, base_density, base_velocity, base_pressure):
    vectors, fields, cells, both, width = adjoint_vectors.shape
    rows = both // 2
    if cells != 4 or vectors != 2 or rows % PAD:
        raise ValueError("unexpected block")
    f32 = jnp.float32
    shape = lambda *s: jax.ShapeDtypeStruct(s, f32)
    tab = jnp.asarray(theta_table(width))
    block, pair = shape(2, 5, cells, rows, width), shape(2, 5, 2, rows, width)
    base, edge = shape(5, cells, rows, width), shape(20 * cells, width)
    halves = lambda a: a.reshape(a.shape[:-2] + (2, rows, width))
    scratch = [
        pltpu.VMEM((2, 5, cells, rows + 2 * PAD, width), f32),
        pltpu.VMEM((2, 5, cells, rows + 2 * PAD, width), f32),
        pltpu.VMEM((2, 5, cells, rows, width), f32),
        pltpu.VMEM((10 * cells * rows, 2 * width), jnp.bfloat16),
        pltpu.VMEM((10 * cells * rows, 2 * width), jnp.bfloat16),
        pltpu.VMEM((2 * cells * rows, width), f32),
    ]
    whole = pltpu.VMEM((2, 5, cells, rows, width), f32)

    gx, row = lax.axis_size("gx"), lax.axis_size("row")
    partner = [(g, g + 1 - 2 * (g % 2)) for g in range(gx)]
    near = [(g, g - 2 + 4 * (g % 2)) for g in range(gx)]
    far = [(g, g + 2 - 4 * (g % 2)) for g in range(gx)]
    inside = lambda perm: [(a, b) for a, b in perm if 0 <= b < gx]
    trade = lambda value: lax.ppermute(value, "gx", partner)
    send_near = lambda value: lax.ppermute(value, "gx", inside(near))
    send_far = lambda value: lax.ppermute(value, "gx", inside(far))

    def beside(value, cross, flip):
        perm = []
        for g in range(gx):
            for j in range(row):
                side = (g + j + flip) % 2
                k = j - 1 + 2 * side
                if 0 <= k < row:
                    perm.append((g * row + j, (partner[g][1] if cross else g) * row + k))
        return lax.ppermute(value, ("gx", "row"), perm)

    def call(kernel, name, outs, ins, extra=(), **more):
        return pl.pallas_call(
            kernel, name=name, out_shape=outs, in_specs=[VM] * len(ins), out_specs=[VM] * len(outs),
            scratch_shapes=list(scratch) + list(extra), compiler_params=PARAMS, **more,
        )(*ins)

    hbm = lambda a: pltpu.with_memory_space_constraint(a, pltpu.HBM)
    own, other, outer, inner, base_own, base_send, table = pl.pallas_call(
        load_kernel, name="load",
        out_shape=[block, block, pair, pair, base, base, jax.ShapeDtypeStruct(tab.shape, tab.dtype)],
        in_specs=[HB] * 5, out_specs=[VM] * 7, scratch_shapes=[pltpu.SemaphoreType.DMA((11,))],
        compiler_params=PARAMS,
    )(hbm(halves(adjoint_vectors)), hbm(halves(base_density)), hbm(halves(base_velocity)),
      hbm(halves(base_pressure)), hbm(tab))
    base_par, outer, inner = trade(base_send), trade(outer), trade(inner)
    part_own, xp_own, xd_own, rp_own, rd_own, rp_other, rd_other = call(
        own_first_kernel, "own_1", [block, pair, pair, edge, edge, edge, edge],
        (own, other, base_own, base_send, table))
    xd_par_in = send_near(xd_own)
    rd_own_in = beside(rd_own, False, 0)
    rd_par_in = beside(rd_other, True, 1)
    rp_par_in = trade(rp_own)
    xd_par = pl.pallas_call(
        face_kernel, name="face", out_shape=pair, in_specs=[VM] * 2, out_specs=VM, compiler_params=PARAMS,
    )(outer, base_par)
    xd_own_in = send_far(xd_par)
    w_par, part_par, xp_par = call(
        partner_first_kernel, "partner_1", [block, block, pair], (outer, inner, base_par, table))
    part_own, xp_own2, xd_own, rp_own, rd_own = call(
        functools.partial(second_kernel, True), "own_2", [block, pair, pair, edge, edge],
        (own, part_own, xp_par, xd_own_in, rp_other, rd_own_in, base_own, table), (whole,))
    xd_par_in2 = send_near(xd_own)
    rd_own_in = beside(rd_own, False, 0)
    inner, outer, xp_par, xd_par, rp_par, rd_par = call(
        second_kernel_par, "partner_2", [pair, pair, pair, pair, edge, edge],
        (w_par, part_par, xp_own, xd_par_in, rp_par_in, rd_par_in, base_par, table, xp_own2), (whole, whole))
    inner = trade(inner)
    xd_own_in = send_far(xd_par)
    rd_other_in = beside(rd_par, True, 0)
    rp_own_in = trade(rp_par)
    outer = trade(pl.pallas_call(
        sum_kernel, name="sum", out_shape=pair, in_specs=[VM] * 2, out_specs=VM, compiler_params=PARAMS,
    )(outer, xd_par_in2))
    full = shape(2, 5, cells, 2, rows, width)
    out = pl.pallas_call(
        own_last_kernel, name="own_3", out_shape=full, in_specs=[VM] * 5, out_specs=HB,
        scratch_shapes=[whole, pltpu.SemaphoreType.DMA], compiler_params=PARAMS,
    )(part_own, xp_par, xd_own_in, rp_own_in, rd_own_in)
    for name, is_outer, back in (("inner_3", False, inner), ("outer_3", True, outer)):
        out = pl.pallas_call(
            functools.partial(other_last_kernel, is_outer), name=name, out_shape=full,
            in_specs=[VM] * 3 + [HB], out_specs=HB,
            scratch_shapes=[pltpu.VMEM((2, 5, 2, rows, width), f32), pltpu.SemaphoreType.DMA],
            input_output_aliases={3: 0}, compiler_params=PARAMS,
        )(back, rp_own, rd_other_in, out)
    return out.reshape(adjoint_vectors.shape)


def solution(mesh):
    in_specs = (
        P(None, None, "gx", "row", None),
        P("gx", "row", None),
        P(None, "gx", "row", None),
        P("gx", "row", None),
    )
    out_specs = P(None, None, "gx", "row", None)
    return jax.shard_map(local, mesh=mesh, in_specs=in_specs, out_specs=out_specs, check_vma=False)
```

```python
import functools

import jax
import jax.numpy as jnp
import ml_dtypes
import numpy as np
from jax import lax
from jax.experimental import pallas as pl
from jax.experimental.pallas import tpu as pltpu
from jax.sharding import PartitionSpec as P

gamma_ratio = 1.4
viscosity = 0.1
time_step = 0.3

A1 = 8.0 / 12.0
A2 = 1.0 / 12.0
B1 = viscosity * 16.0 / 12.0
B2 = viscosity / 12.0
CENTRE = -2.0 * viscosity * 30.0 / 12.0
PAD = 8


def theta_table(azimuth):
    spacing = 2.0 * np.pi / azimuth
    index = np.arange(azimuth)
    offset = index[:, None] - index[None, :]
    signs = np.where(offset % 2 == 0, 1.0, -1.0)
    angle = offset * (spacing / 2.0)
    diagonal = offset == 0
    tangent = np.where(diagonal, 1.0, np.tan(angle))
    sine = np.where(diagonal, 1.0, np.sin(angle))
    first = np.where(diagonal, 0.0, 0.5 * signs * spacing / tangent)
    second = np.where(
        diagonal, -(np.pi**2) / 3.0 - spacing**2 / 6.0, -0.5 * signs * spacing**2 / (sine * sine)
    )
    table = np.concatenate([first.T, viscosity * second.T], axis=0).astype(np.float32)
    high = table.astype(ml_dtypes.bfloat16)
    low = (table - high.astype(np.float32)).astype(ml_dtypes.bfloat16)
    return np.concatenate([high, low], axis=1)


def fluxes(base_ref, c, at, w, directions):
    rho, pr = base_ref[0, c, at], base_ref[4, c, at]
    inv = 1.0 / rho
    pg = gamma_ratio * pr
    flows = []
    for v in range(2):
        q = rho * w[v][0] + pg * w[v][4]
        rows = []
        for d in directions:
            speed = base_ref[1 + d, c, at]
            flow = [speed * w[v][f] for f in range(5)]
            flow[1 + d] = flow[1 + d] + q
            flow[4] = flow[4] + w[v][1 + d] * inv
            rows.append(flow)
        flows.append(rows)
    return flows


def radial(fr, wp, v, f, c, r, n):
    base = PAD + r
    sh = lambda buf, k: buf[v, f, c, base + k : base + k + n]
    return (
        A1 * (sh(fr, 1) - sh(fr, -1))
        - A2 * (sh(fr, 2) - sh(fr, -2))
        + B1 * (sh(wp, 1) + sh(wp, -1))
        - B2 * (sh(wp, 2) + sh(wp, -2))
    )


def clear_pads(fr, wp):
    _, _, cells, padded, width = fr.shape
    zeros = jnp.zeros((PAD, width), jnp.float32)
    for v in range(2):
        for f in range(5):
            for c in range(cells):
                for buf in (wp, fr):
                    buf[v, f, c, 0:PAD] = zeros
                    buf[v, f, c, padded - PAD : padded] = zeros


def put_edges(dt, line, fr, wp, rp_ref, rd_ref):
    _, _, cells, padded, _ = fr.shape
    for v in range(2):
        for f in range(5):
            for c in range(cells):
                low = dt * radial(fr, wp, v, f, c, -2, 2)
                high = dt * radial(fr, wp, v, f, c, padded - 2 * PAD, 2)
                k = 2 * ((5 * v + f) * cells + c)
                rp_ref[k : k + 2] = jnp.where(line == 0, high, low)
                rd_ref[k : k + 2] = jnp.where(line == 0, low, high)


def section(dt, parity, line, half, get, start, base_ref, tab_ref, put, xp_ref, xd_ref, rp_ref, rd_ref,
            wp, fr, fx, xh, xl, ys):
    _, cells, rows, width = base_ref.shape
    total_rows = 2 * rows * lax.axis_size("row")
    row_start = lax.axis_index("row") * (2 * rows) + half * rows
    span = 2 * cells * rows
    clear_pads(fr, wp)

    def split(flow, k, lanes):
        both = jnp.concatenate(flow, axis=0)
        high = both.astype(jnp.bfloat16)
        xh[k : k + 2 * PAD, lanes] = high
        xl[k : k + 2 * PAD, lanes] = (both - high.astype(jnp.float32)).astype(jnp.bfloat16)

    for r in range(0, rows, PAD):
        at = slice(r, r + PAD)
        inside = slice(PAD + r, 2 * PAD + r)
        index = row_start + r + lax.broadcasted_iota(jnp.int32, (PAD, width), 0)
        fac = 1.0 / (1.0 + (index.astype(jnp.float32) + 0.5) / total_rows)
        for c in range(cells):
            w = [[get(v, f, c, r) for f in range(5)] for v in range(2)]
            flows = fluxes(base_ref, c, at, w, (0, 1, 2))
            for f in range(5):
                k = f * span + (c * (rows // PAD) + r // PAD) * 2 * PAD
                for v in range(2):
                    fx[v, f, c, at] = flows[v][0][f]
                    fr[v, f, c, inside] = flows[v][1][f]
                    wp[v, f, c, inside] = w[v][f]
                split([flows[v][2][f] * fac for v in range(2)], k, slice(0, width))
                split([w[v][f] for v in range(2)], k, slice(width, 2 * width))
    for f in range(5):
        both = jnp.dot(xh[f * span : (f + 1) * span], tab_ref[...], preferred_element_type=jnp.float32)
        low = jnp.dot(xl[f * span : (f + 1) * span], tab_ref[:, 0:width], preferred_element_type=jnp.float32)
        ys[...] = (both[:, 0:width] + both[:, width:]) + low
        for v in range(2):
            for r in range(0, rows, PAD):
                at = slice(r, r + PAD)
                ws = [wp[v, f, c, PAD + r : 2 * PAD + r] for c in range(cells)]
                fs = [fx[v, f, c, at] for c in range(cells)]

                def stream(i):
                    total = None
                    for k, a, b in ((1, A1, B1), (-1, -A1, B1), (2, -A2, -B2), (-2, A2, -B2)):
                        if 0 <= i + k < cells:
                            term = a * fs[i + k] + b * ws[i + k]
                            total = term if total is None else total + term
                    return total

                for j in range(2):
                    low_face = dt * stream(j - 2)
                    high_face = dt * stream(cells + j)
                    xp_ref[v, f, j, at] = jnp.where(parity == 0, high_face, low_face)
                    if xd_ref is not None:
                        xd_ref[v, f, j, at] = jnp.where(parity == 0, low_face, high_face)
                for c in range(cells):
                    k = (c * (rows // PAD) + r // PAD) * 2 * PAD + PAD * v
                    total = stream(c) + radial(fr, wp, v, f, c, r, PAD) + CENTRE * ws[c] + ys[k : k + PAD]
                    put(v, f, c, at, start(v, f, c, r) + dt * total)
    if rp_ref is not None:
        put_edges(dt, line, fr, wp, rp_ref, rd_ref)


def add_edges(line, rp_ref, rd_ref, out, cells):
    rows = out.shape[3]
    for v in range(2):
        for f in range(5):
            for c, place in cells:
                k = 2 * ((5 * v + f) * 4 + c)
                if not isinstance(c, int):
                    k = pl.multiple_of(k, 2)
                rp, rd = rp_ref[pl.ds(k, 2)], rd_ref[pl.ds(k, 2)]
                out[v, f, place, 0:2] += jnp.where(line == 0, rd, rp)
                out[v, f, place, rows - 2 : rows] += jnp.where(line == 0, rp, rd)


def add_faces(parity, xp_ref, xd_ref, out):
    cells = out.shape[2]
    for v in range(2):
        for f in range(5):
            for j in range(2):
                out[v, f, (cells - 2) * (1 - parity) + j] += xp_ref[v, f, j]
                out[v, f, (cells - 2) * parity + j] += xd_ref[v, f, j]


def all_cells(fn):
    for v in range(2):
        for f in range(5):
            for c in range(4):
                fn(v, f, c)


def place():
    column = lax.axis_index("gx") % 2
    return column, (column + lax.axis_index("row")) % 2


def load_kernel(w_hbm, rho_hbm, vel_hbm, pr_hbm, tab_hbm,
                own_ref, other_ref, outer_ref, inner_ref, base_ref, send_ref, tab_ref, sems):
    column, half = place()
    outer = 2 * column
    pairs = []
    for side, ref in ((1 - half, send_ref), (half, base_ref)):
        pairs.append((rho_hbm.at[:, side], ref.at[0]))
        pairs.append((vel_hbm.at[:, :, side], ref.at[1:4]))
        pairs.append((pr_hbm.at[:, side], ref.at[4]))
    pairs.append((w_hbm.at[:, :, pl.ds(outer, 2), 1 - half], outer_ref))
    pairs.append((w_hbm.at[:, :, pl.ds(2 - outer, 2), 1 - half], inner_ref))
    pairs.append((w_hbm.at[:, :, :, half], own_ref))
    pairs.append((w_hbm.at[:, :, :, 1 - half], other_ref))
    pairs.append((tab_hbm, tab_ref))
    copies = [pltpu.make_async_copy(a, b, sems.at[i]) for i, (a, b) in enumerate(pairs)]
    for copy in copies:
        copy.start()
    for copy in copies:
        copy.wait()


def own_first_kernel(own_ref, other_ref, base_ref, send_ref, tab_ref,
                     part_ref, xp_ref, xd_ref, rp_ref, rd_ref, rpo_ref, rdo_ref, wp, fr, *scratch):
    column, half = place()
    _, cells, rows, _ = base_ref.shape
    get = lambda v, f, c, r: own_ref[v, f, c, r : r + PAD]

    def put(v, f, c, at, value):
        part_ref[v, f, c, at] = value

    section(0.5 * time_step, column, half, half, get, get, base_ref, tab_ref, put,
            xp_ref, xd_ref, rp_ref, rd_ref, wp, fr, *scratch)
    for c in range(cells):
        for r in (0, rows - PAD):
            w = [[other_ref[v, f, c, r : r + PAD] for f in range(5)] for v in range(2)]
            flows = fluxes(send_ref, c, slice(r, r + PAD), w, (1,))
            for v in range(2):
                for f in range(5):
                    fr[v, f, c, PAD + r : 2 * PAD + r] = flows[v][0][f]
                    wp[v, f, c, PAD + r : 2 * PAD + r] = w[v][f]
    put_edges(0.5 * time_step, 1 - half, fr, wp, rpo_ref, rdo_ref)


def face_kernel(outer_ref, base_ref, _, own_ref, xd_ref, copy_ref):
    column, _ = place()
    parity = 1 - column
    dt = 0.5 * time_step
    copy_ref[...] = own_ref[...]
    rows = outer_ref.shape[3]
    for r in range(0, rows, PAD):
        at = slice(r, r + PAD)
        w = [[[outer_ref[v, f, j, at] for f in range(5)] for v in range(2)] for j in range(2)]
        flows = [fluxes(base_ref, 2 * parity + j, at, w[j], (0,)) for j in range(2)]
        for v in range(2):
            for f in range(5):
                f0, f1 = flows[0][v][0][f], flows[1][v][0][f]
                w0, w1 = w[0][v][f], w[1][v][f]
                low = (-A2 * f0 - B2 * w0, (A1 * f0 + B1 * w0) + (-A2 * f1 - B2 * w1))
                high = ((-A1 * f1 + B1 * w1) + (A2 * f0 - B2 * w0), A2 * f1 - B2 * w1)
                for j in range(2):
                    xd_ref[v, f, j, at] = dt * jnp.where(parity == 0, low[j], high[j])


def pack_kernel(inner_ref, rp_ref, rd_ref, _, message_ref):
    rows = inner_ref.shape[3]
    for v in range(2):
        for f in range(5):
            for j in range(2):
                k = ((5 * v + f) * 2 + j) * rows
                message_ref[k : k + rows] = inner_ref[v, f, j]
    n = 20 * rows
    edge = rp_ref.shape[0]
    message_ref[n : n + edge] = rp_ref[...]
    message_ref[n + edge : n + 2 * edge] = rd_ref[...]


def partner_first_kernel(outer_ref, message_ref, base_ref, tab_ref, w_ref, part_ref, xp_ref, *scratch):
    column, half = place()
    parity = 1 - column
    rows = outer_ref.shape[3]
    for v in range(2):
        for f in range(5):
            for j in range(2):
                w_ref[v, f, 2 * parity + j] = outer_ref[v, f, j]
                k = ((5 * v + f) * 2 + j) * rows
                w_ref[v, f, 2 - 2 * parity + j] = message_ref[k : k + rows]
    get = lambda v, f, c, r: w_ref[v, f, c, r : r + PAD]

    def put(v, f, c, at, value):
        part_ref[v, f, c, at] = value

    section(0.5 * time_step, parity, half, half, get, get, base_ref, tab_ref, put,
            xp_ref, None, None, None, *scratch)


def start_second(parity, half, part_ref, xp_in, xd_in, rp_in, rd_in, s1):
    def fill(v, f, c):
        s1[v, f, c] = part_ref[v, f, c]

    all_cells(fill)
    add_faces(parity, xp_in, xd_in, s1)
    add_edges(half, rp_in, rd_in, s1, [(c, c) for c in range(4)])


def own_second_kernel(w_ref, part_ref, xp_in, xd_in, rp_in, rd_in, base_ref, tab_ref,
                      out_ref, xp_ref, xd_ref, rp_ref, rd_ref, *scratch):
    *scratch, s1 = scratch
    column, half = place()
    start_second(column, half, part_ref, xp_in, xd_in, rp_in, rd_in, s1)
    get = lambda v, f, c, r: s1[v, f, c, r : r + PAD]
    start = lambda v, f, c, r: w_ref[v, f, c, r : r + PAD]

    def put(v, f, c, at, value):
        out_ref[v, f, c, at] = value

    section(time_step, column, half, half, get, start, base_ref, tab_ref, put,
            xp_ref, xd_ref, rp_ref, rd_ref, *scratch)


def partner_second_kernel(w_ref, part_ref, xp_in, xd_in, message_in, xp_own, base_ref, tab_ref,
                          message_ref, outer_ref, xp_ref, xd_ref, rd_ref, *scratch):
    *scratch, s1, target = scratch
    column, half = place()
    parity = 1 - column
    rows = outer_ref.shape[3]
    n = 20 * rows
    edge = rd_ref.shape[0]
    start_second(parity, half, part_ref, xp_in, xd_in, message_in.at[n : n + edge],
                 message_in.at[n + edge : n + 2 * edge], s1)
    get = lambda v, f, c, r: s1[v, f, c, r : r + PAD]
    start = lambda v, f, c, r: w_ref[v, f, c, r : r + PAD]

    def put(v, f, c, at, value):
        target[v, f, c, at] = value

    section(time_step, parity, half, half, get, start, base_ref, tab_ref, put,
            xp_ref, xd_ref, message_ref.at[n : n + edge], rd_ref, *scratch)
    for v in range(2):
        for f in range(5):
            for j in range(2):
                k = ((5 * v + f) * 2 + j) * rows
                message_ref[k : k + rows] = target[v, f, 2 - 2 * parity + j] + xp_own[v, f, j]
                outer_ref[v, f, j] = target[v, f, 2 * parity + j]


def finish_kernel(outer_ref, xd_ref, message_ref):
    message_ref[...] = outer_ref[...] + xd_ref[...]


def own_last_kernel(part_ref, xp_ref, xd_ref, message_ref, rd_ref, out_hbm, value, sem):
    column, half = place()
    edge = rd_ref.shape[0]
    n = message_ref.shape[0] - edge
    start_second(column, half, part_ref, xp_ref, xd_ref, message_ref.at[n : n + edge], rd_ref, value)
    copy = pltpu.make_async_copy(value, out_hbm.at[:, :, :, half], sem)
    copy.start()
    copy.wait()


def other_last_kernel(inner_ref, outer_ref, rp_ref, rd_ref, _, out_hbm, value, sem):
    column, half = place()
    rows = value.shape[3]
    for v in range(2):
        for f in range(5):
            for j in range(2):
                k = ((5 * v + f) * 2 + j) * rows
                value[v, f, 2 * column + j] = outer_ref[v, f, j]
                value[v, f, 2 - 2 * column + j] = inner_ref[k : k + rows]
    add_edges(1 - half, rp_ref, rd_ref, value, [(c, c) for c in range(4)])
    copy = pltpu.make_async_copy(value, out_hbm.at[:, :, :, 1 - half], sem)
    copy.start()
    copy.wait()


VM = pl.BlockSpec(memory_space=pltpu.VMEM)
HB = pl.BlockSpec(memory_space=pltpu.HBM)
PARAMS = pltpu.CompilerParams(vmem_limit_bytes=40 << 20)


def local(adjoint_vectors, base_density, base_velocity, base_pressure):
    vectors, fields, cells, both, width = adjoint_vectors.shape
    rows = both // 2
    if cells != 4 or vectors != 2 or rows % PAD:
        raise ValueError("unexpected block")
    f32 = jnp.float32
    shape = lambda *s: jax.ShapeDtypeStruct(s, f32)
    tab = jnp.asarray(theta_table(width))
    block, pair = shape(2, 5, cells, rows, width), shape(2, 5, 2, rows, width)
    base, edge = shape(5, cells, rows, width), shape(20 * cells, width)
    halves = lambda a: a.reshape(a.shape[:-2] + (2, rows, width))
    scratch = [
        pltpu.VMEM((2, 5, cells, rows + 2 * PAD, width), f32),
        pltpu.VMEM((2, 5, cells, rows + 2 * PAD, width), f32),
        pltpu.VMEM((2, 5, cells, rows, width), f32),
        pltpu.VMEM((10 * cells * rows, 2 * width), jnp.bfloat16),
        pltpu.VMEM((10 * cells * rows, 2 * width), jnp.bfloat16),
        pltpu.VMEM((2 * cells * rows, width), f32),
    ]
    whole = pltpu.VMEM((2, 5, cells, rows, width), f32)

    gx, row = lax.axis_size("gx"), lax.axis_size("row")
    partner = [(g, g + 1 - 2 * (g % 2)) for g in range(gx)]
    near = [(g, g - 2 + 4 * (g % 2)) for g in range(gx)]
    far = [(g, g + 2 - 4 * (g % 2)) for g in range(gx)]
    inside = lambda perm: [(a, b) for a, b in perm if 0 <= b < gx]
    trade = lambda value: lax.ppermute(value, "gx", partner)
    send_near = lambda value: lax.ppermute(value, "gx", inside(near))
    send_far = lambda value: lax.ppermute(value, "gx", inside(far))

    def beside(value, cross, flip):
        perm = []
        for g in range(gx):
            for j in range(row):
                side = (g + j + flip) % 2
                k = j - 1 + 2 * side
                if 0 <= k < row:
                    perm.append((g * row + j, (partner[g][1] if cross else g) * row + k))
        return lax.ppermute(value, ("gx", "row"), perm)

    def call(kernel, name, outs, ins, extra=(), **more):
        return pl.pallas_call(
            kernel, name=name, out_shape=outs, in_specs=[VM] * len(ins), out_specs=[VM] * len(outs),
            scratch_shapes=list(scratch) + list(extra), compiler_params=PARAMS, **more,
        )(*ins)

    hbm = lambda a: pltpu.with_memory_space_constraint(a, pltpu.HBM)
    own, other, outer, inner, base_own, base_send, table = pl.pallas_call(
        load_kernel, name="load",
        out_shape=[block, block, pair, pair, base, base, jax.ShapeDtypeStruct(tab.shape, tab.dtype)],
        in_specs=[HB] * 5, out_specs=[VM] * 7, scratch_shapes=[pltpu.SemaphoreType.DMA((11,))],
        compiler_params=PARAMS,
    )(hbm(halves(adjoint_vectors)), hbm(halves(base_density)), hbm(halves(base_velocity)),
      hbm(halves(base_pressure)), hbm(tab))
    small = lambda kernel, name, outs, *ins: pl.pallas_call(
        kernel, name=name, out_shape=outs, in_specs=[VM] * len(ins), out_specs=VM, compiler_params=PARAMS)(*ins)
    outer, base_par = trade(outer), trade(base_send)
    part_own, xp_own, xd_own, rp_own, rd_own, rp_other, rd_other = call(
        own_first_kernel, "own_1", [block, pair, pair, edge, edge, edge, edge],
        (own, other, base_own, base_send, table))
    rd_own_in = beside(rd_own, False, 0)
    rd_other_in = beside(rd_other, False, 1)
    n, e = 20 * rows, 20 * cells
    packed = small(pack_kernel, "pack", shape(n + 2 * e, width), inner, rp_own, rd_other_in, rd_own_in)
    message = trade(packed)
    xd_par, xd_own = pl.pallas_call(
        face_kernel, name="face", out_shape=[pair, pair], in_specs=[VM] * 4, out_specs=[VM] * 2, compiler_params=PARAMS,
    )(outer, base_par, packed, xd_own)
    xd_own_in, xd_par_in = send_far(xd_par), send_near(xd_own)
    w_par, part_par, xp_par = call(
        partner_first_kernel, "partner_1", [block, block, pair], (outer, message, base_par, table))
    part_own, xp_own2, xd_own, rp_own, rd_own = call(
        own_second_kernel, "own_2", [block, pair, pair, edge, edge],
        (own, part_own, xp_par, xd_own_in, rp_other, rd_own_in, base_own, table), (whole,))
    xd_par_in2 = send_near(xd_own)
    inner, outer, xp_par, xd_par, rd_par = call(
        partner_second_kernel, "partner_2", [shape(n + e, width), pair, pair, pair, edge],
        (w_par, part_par, xp_own, xd_par_in, message, xp_own2, base_par, table), (whole, whole))
    inner = trade(inner)
    outer = trade(small(finish_kernel, "finish", pair, outer, xd_par_in2))
    xd_own_in = send_far(xd_par)
    rd_other_in = beside(rd_par, True, 0)
    rd_own_in = beside(rd_own, False, 0)
    full = shape(2, 5, cells, 2, rows, width)
    last = dict(out_shape=full, out_specs=HB, scratch_shapes=[whole, pltpu.SemaphoreType.DMA], compiler_params=PARAMS)
    out = pl.pallas_call(own_last_kernel, name="own_3", in_specs=[VM] * 5, **last)(
        part_own, xp_par, xd_own_in, inner, rd_own_in)
    out = pl.pallas_call(
        other_last_kernel, name="other_3", in_specs=[VM] * 4 + [HB], input_output_aliases={4: 0}, **last,
    )(inner, outer, rp_own, rd_other_in, out)
    return out.reshape(adjoint_vectors.shape)


def solution(mesh):
    in_specs = (
        P(None, None, "gx", "row", None),
        P("gx", "row", None),
        P(None, "gx", "row", None),
        P("gx", "row", None),
    )
    out_specs = P(None, None, "gx", "row", None)
    return jax.shard_map(local, mesh=mesh, in_specs=in_specs, out_specs=out_specs, check_vma=False)
```

```python
import functools

import jax
import jax.numpy as jnp
import ml_dtypes
import numpy as np
from jax import lax
from jax.experimental import pallas as pl
from jax.experimental.pallas import tpu as pltpu
from jax.sharding import PartitionSpec as P

gamma_ratio = 1.4
viscosity = 0.1
time_step = 0.3

A1 = 8.0 / 12.0
A2 = 1.0 / 12.0
B1 = viscosity * 16.0 / 12.0
B2 = viscosity / 12.0
CENTRE = -2.0 * viscosity * 30.0 / 12.0
PAD = 8


def theta_table(azimuth):
    spacing = 2.0 * np.pi / azimuth
    index = np.arange(azimuth)
    offset = index[:, None] - index[None, :]
    signs = np.where(offset % 2 == 0, 1.0, -1.0)
    angle = offset * (spacing / 2.0)
    diagonal = offset == 0
    tangent = np.where(diagonal, 1.0, np.tan(angle))
    sine = np.where(diagonal, 1.0, np.sin(angle))
    first = np.where(diagonal, 0.0, 0.5 * signs * spacing / tangent)
    second = np.where(
        diagonal, -(np.pi**2) / 3.0 - spacing**2 / 6.0, -0.5 * signs * spacing**2 / (sine * sine)
    )
    table = np.concatenate([first.T, viscosity * second.T], axis=0).astype(np.float32)
    high = table.astype(ml_dtypes.bfloat16)
    low = (table - high.astype(np.float32)).astype(ml_dtypes.bfloat16)
    return np.concatenate([high, low], axis=1)


def fluxes(base_ref, c, at, w, directions):
    rho, pr = base_ref[0, c, at], base_ref[4, c, at]
    inv = 1.0 / rho
    pg = gamma_ratio * pr
    flows = []
    for v in range(2):
        q = rho * w[v][0] + pg * w[v][4]
        rows = []
        for d in directions:
            speed = base_ref[1 + d, c, at]
            flow = [speed * w[v][f] for f in range(5)]
            flow[1 + d] = flow[1 + d] + q
            flow[4] = flow[4] + w[v][1 + d] * inv
            rows.append(flow)
        flows.append(rows)
    return flows


def radial(fr, wp, v, f, c, r, n):
    base = PAD + r
    sh = lambda buf, k: buf[v, f, c, base + k : base + k + n]
    near = 8.0 * (sh(fr, 1) - sh(fr, -1)) - (sh(fr, 2) - sh(fr, -2))
    return near + B1 * (sh(wp, 1) + sh(wp, -1)) - B2 * (sh(wp, 2) + sh(wp, -2))


def clear_pads(fr, wp):
    _, _, cells, padded, width = fr.shape
    zeros = jnp.zeros((PAD, width), jnp.float32)
    for v in range(2):
        for f in range(5):
            for c in range(cells):
                for buf in (wp, fr):
                    buf[v, f, c, 0:PAD] = zeros
                    buf[v, f, c, padded - PAD : padded] = zeros


def put_edges(dt, line, fr, wp, rp_ref, rd_ref):
    _, _, cells, padded, _ = fr.shape
    for v in range(2):
        for f in range(5):
            for c in range(cells):
                low = dt * radial(fr, wp, v, f, c, -2, 2)
                high = dt * radial(fr, wp, v, f, c, padded - 2 * PAD, 2)
                k = 2 * ((5 * v + f) * cells + c)
                rp_ref[k : k + 2] = jnp.where(line == 0, high, low)
                rd_ref[k : k + 2] = jnp.where(line == 0, low, high)


def section(dt, parity, line, half, get, start, base_ref, tab_ref, put, xp_ref, xd_ref, rp_ref, rd_ref,
            wp, fr, fx, xh, xl, ys):
    _, cells, rows, width = base_ref.shape
    total_rows = 2 * rows * lax.axis_size("row")
    row_start = lax.axis_index("row") * (2 * rows) + half * rows
    span = 2 * cells * rows
    clear_pads(fr, wp)

    def split(flow, k, lanes):
        both = jnp.concatenate(flow, axis=0)
        high = both.astype(jnp.bfloat16)
        xh[k : k + 2 * PAD, lanes] = high
        xl[k : k + 2 * PAD, lanes] = (both - high.astype(jnp.float32)).astype(jnp.bfloat16)

    for r in range(0, rows, PAD):
        at = slice(r, r + PAD)
        inside = slice(PAD + r, 2 * PAD + r)
        index = row_start + r + lax.broadcasted_iota(jnp.int32, (PAD, width), 0)
        fac = 1.0 / (1.0 + (index.astype(jnp.float32) + 0.5) / total_rows)
        for c in range(cells):
            w = [[get(v, f, c, r) for f in range(5)] for v in range(2)]
            flows = fluxes(base_ref, c, at, w, (0, 1, 2))
            for f in range(5):
                k = f * span + (c * (rows // PAD) + r // PAD) * 2 * PAD
                for v in range(2):
                    fx[v, f, c, at] = A2 * flows[v][0][f]
                    fr[v, f, c, inside] = A2 * flows[v][1][f]
                    wp[v, f, c, inside] = w[v][f]
                split([flows[v][2][f] * fac for v in range(2)], k, slice(0, width))
                split([w[v][f] for v in range(2)], k, slice(width, 2 * width))
    both = jnp.dot(xh[...], tab_ref[...], preferred_element_type=jnp.float32)
    low = jnp.dot(xl[...], tab_ref[:, 0:width], preferred_element_type=jnp.float32)
    ys[...] = (both[:, 0:width] + both[:, width:]) + low
    for f in range(5):
        for v in range(2):
            for r in range(0, rows, PAD):
                at = slice(r, r + PAD)
                ws = [wp[v, f, c, PAD + r : 2 * PAD + r] for c in range(cells)]
                fs = [fx[v, f, c, at] for c in range(cells)]
                small = [B2 * w for w in ws]
                far_left = [a - b for a, b in zip(fs, small)]
                far_right = [-a - b for a, b in zip(fs, small)]
                large, steep = [16.0 * b for b in small], [8.0 * a for a in fs]
                left = [b - a for a, b in zip(steep, large)]
                right = [b + a for a, b in zip(steep, large)]

                def stream(i):
                    total = None
                    for k, terms in ((1, right), (-1, left), (2, far_right), (-2, far_left)):
                        if 0 <= i + k < cells:
                            total = terms[i + k] if total is None else total + terms[i + k]
                    return total

                for j in range(2 if xp_ref is not None else 0):
                    low_face = dt * stream(j - 2)
                    high_face = dt * stream(cells + j)
                    xp_ref[v, f, j, at] = jnp.where(parity == 0, high_face, low_face)
                    if xd_ref is not None:
                        xd_ref[v, f, j, at] = jnp.where(parity == 0, low_face, high_face)
                for c in range(cells):
                    k = f * span + (c * (rows // PAD) + r // PAD) * 2 * PAD + PAD * v
                    total = stream(c) + radial(fr, wp, v, f, c, r, PAD) + CENTRE * ws[c] + ys[k : k + PAD]
                    put(v, f, c, at, start(v, f, c, r) + dt * total)
    if rp_ref is not None:
        put_edges(dt, line, fr, wp, rp_ref, rd_ref)


def add_edges(line, rp_ref, rd_ref, out, cells):
    rows = out.shape[3]
    for v in range(2):
        for f in range(5):
            for c, place in cells:
                k = 2 * ((5 * v + f) * 4 + c)
                if not isinstance(c, int):
                    k = pl.multiple_of(k, 2)
                rp, rd = rp_ref[pl.ds(k, 2)], rd_ref[pl.ds(k, 2)]
                out[v, f, place, 0:2] += jnp.where(line == 0, rd, rp)
                out[v, f, place, rows - 2 : rows] += jnp.where(line == 0, rp, rd)


def add_faces(parity, xp_ref, xd, out):
    cells = out.shape[2]
    for v in range(2):
        for f in range(5):
            for j in range(2):
                out[v, f, (cells - 2) * (1 - parity) + j] += xp_ref[v, f, j]
                out[v, f, (cells - 2) * parity + j] += xd(v, f, j)


def all_cells(fn):
    for v in range(2):
        for f in range(5):
            for c in range(4):
                fn(v, f, c)


def pick(which, first_ref, second_ref):
    return lambda *at: jnp.where(which == 0, first_ref[at], second_ref[at])


def z_side():
    return (lax.axis_index("gx") // 2 + lax.axis_index("gx")) % 2


def place():
    column = lax.axis_index("gx") % 2
    return column, (column + lax.axis_index("row")) % 2


def load_kernel(w_hbm, rho_hbm, vel_hbm, pr_hbm, tab_hbm,
                own_ref, other_ref, outer_ref, base_ref, send_ref, rest_ref, tab_ref, sems):
    column, half = place()
    outer, inner = pl.ds(2 * column, 2), pl.ds(2 - 2 * column, 2)
    side = 1 - half
    pairs = []
    for v in range(2):
        for f in range(5):
            k = 2 * (5 * v + f)
            pairs.append((w_hbm.at[v, f, outer, side], outer_ref.at[k : k + 2]))
            pairs.append((w_hbm.at[v, f, inner, side], rest_ref.at[14 + k : 16 + k]))
    for ref, first, cells in ((outer_ref, 20, outer), (rest_ref, 0, inner)):
        pairs.append((rho_hbm.at[cells, side], ref.at[first : first + 2]))
        pairs.append((vel_hbm.at[0, cells, side], ref.at[first + 2 : first + 4]))
        pairs.append((pr_hbm.at[cells, side], ref.at[first + 4 : first + 6]))
    pairs.append((vel_hbm.at[1, :, side], rest_ref.at[6:10]))
    pairs.append((vel_hbm.at[2, :, side], rest_ref.at[10:14]))
    for part, ref in ((half, base_ref), (side, send_ref)):
        pairs.append((rho_hbm.at[:, part], ref.at[0]))
        pairs.append((vel_hbm.at[:, :, part], ref.at[1:4]))
        pairs.append((pr_hbm.at[:, part], ref.at[4]))
    pairs.append((w_hbm.at[:, :, :, half], own_ref))
    pairs.append((w_hbm.at[:, :, :, side], other_ref))
    pairs.append((tab_hbm, tab_ref))
    copies = [pltpu.make_async_copy(a, b, sems.at[i]) for i, (a, b) in enumerate(pairs)]
    for copy in copies:
        copy.start()
    for copy in copies:
        copy.wait()


def own_first_kernel(own_ref, other_ref, base_ref, send_ref, tab_ref,
                     part_ref, xp_ref, xd_ref, rp_ref, rd_ref, rpo_ref, rdo_ref, wp, fr, *scratch):
    *scratch, rd_own, rd_other = scratch
    column, half = place()
    _, cells, rows, _ = base_ref.shape
    get = lambda v, f, c, r: own_ref[v, f, c, r : r + PAD]

    def put(v, f, c, at, value):
        part_ref[v, f, c, at] = value

    section(0.5 * time_step, column, half, half, get, get, base_ref, tab_ref, put,
            xp_ref, xd_ref, rp_ref, rd_own, wp, fr, *scratch)
    for c in range(cells):
        for r in (0, rows - PAD):
            w = [[other_ref[v, f, c, r : r + PAD] for f in range(5)] for v in range(2)]
            flows = fluxes(send_ref, c, slice(r, r + PAD), w, (1,))
            for v in range(2):
                for f in range(5):
                    fr[v, f, c, PAD + r : 2 * PAD + r] = A2 * flows[v][0][f]
                    wp[v, f, c, PAD + r : 2 * PAD + r] = w[v][f]
    put_edges(0.5 * time_step, 1 - half, fr, wp, rpo_ref, rd_other)
    rd_ref[...] = jnp.where(column == 0, rd_other[...], rd_own[...])
    rdo_ref[...] = jnp.where(column == 0, rd_own[...], rd_other[...])


def pair_face(dt, high_side, v, w, base, put):
    flows = []
    for j in range(2):
        rho, speed, pr = base[j]
        flow = [speed * w[j][f] for f in range(5)]
        flow[1] = flow[1] + (rho * w[j][0] + gamma_ratio * pr * w[j][4])
        flow[4] = flow[4] + w[j][1] / rho
        flows.append(flow)
    for f in range(5):
        f0, f1, w0, w1 = flows[0][f], flows[1][f], w[0][f], w[1][f]
        low = (-A2 * f0 - B2 * w0, (A1 * f0 + B1 * w0) + (-A2 * f1 - B2 * w1))
        high = ((-A1 * f1 + B1 * w1) + (A2 * f0 - B2 * w0), A2 * f1 - B2 * w1)
        for j in range(2):
            put(v, f, j, dt * jnp.where(high_side, high[j], low[j]))


def face_kernel(outer_ref, own_ref, _, first_ref, second_ref):
    column, _ = place()
    rows = outer_ref.shape[1]
    for r in range(0, rows, PAD):
        at = slice(r, r + PAD)
        base = [[outer_ref[20 + 2 * i + j, at] for i in range(3)] for j in range(2)]

        def put(v, f, j, value):
            own = own_ref[v, f, j, at]
            first_ref[v, f, j, at] = jnp.where(z_side() == 0, value, own)
            second_ref[v, f, j, at] = jnp.where(z_side() == 0, own, value)

        for v in range(2):
            w = [[outer_ref[2 * (5 * v + f) + j, at] for f in range(5)] for j in range(2)]
            pair_face(0.5 * time_step, column == 0, v, w, base, put)


def second_face(parity, outer, part_ref, x_in, rp_in, rd_in, base_ref, put, s2):
    _, half = place()
    first = 2 * parity if outer else 2 - 2 * parity
    rows = part_ref.shape[3]
    for v in range(2):
        for f in range(5):
            for j in range(2):
                s2[v, f, j] = part_ref[v, f, first + j] + x_in(v, f, j)
    add_edges(half, rp_in, rd_in, s2, [(first + j, j) for j in range(2)])
    for r in range(0, rows, PAD):
        at = slice(r, r + PAD)
        base = [[base_ref[i, first + j, at] for i in (0, 1, 4)] for j in range(2)]
        for v in range(2):
            w = [[s2[v, f, j, at] for f in range(5)] for j in range(2)]
            pair_face(time_step, (parity == 1) if outer else (parity == 0), v, w, base,
                      lambda v, f, j, value: put(v, f, j, at, value))


def outer_faces_kernel(part_own, part_par, first_in, second_in, rp_own, rd_own, message_in, base_own, base_par,
                       first_ref, second_ref, s2, face):
    column, _ = place()
    side = z_side()
    edge = rp_own.shape[0]

    def keep(v, f, j, at, value):
        face[v, f, j, at] = value

    def put(v, f, j, at, value):
        own = face[v, f, j, at]
        first_ref[v, f, j, at] = jnp.where(side == 0, value, own)
        second_ref[v, f, j, at] = jnp.where(side == 0, own, value)

    second_face(column, True, part_own, pick(side, second_in, first_in), rp_own, rd_own, base_own, keep, s2)
    second_face(1 - column, True, part_par, pick(side, first_in, second_in), message_in.at[0:edge],
                message_in.at[edge : 2 * edge], base_par, put, s2)


def pack_kernel(rp_ref, first_ref, second_ref, message_ref, rd_ref):
    column, _ = place()
    edge = rp_ref.shape[0]
    message_ref[0:edge] = rp_ref[...]
    message_ref[edge : 2 * edge] = jnp.where(column == 0, first_ref[...], second_ref[...])
    rd_ref[...] = jnp.where(column == 0, second_ref[...], first_ref[...])


def partner_first_kernel(outer_ref, rest_ref, tab_ref, w_ref, base_ref, part_ref, xp_ref, *scratch):
    column, half = place()
    parity = 1 - column
    first, second = 2 * parity, 2 - 2 * parity
    for j in range(2):
        for v in range(2):
            for f in range(5):
                k = 2 * (5 * v + f) + j
                w_ref[v, f, first + j] = outer_ref[k]
                w_ref[v, f, second + j] = rest_ref[14 + k]
        for i, field in enumerate((0, 1, 4)):
            base_ref[field, first + j] = outer_ref[20 + 2 * i + j]
            base_ref[field, second + j] = rest_ref[2 * i + j]
    for c in range(4):
        base_ref[2, c] = rest_ref[6 + c]
        base_ref[3, c] = rest_ref[10 + c]
    get = lambda v, f, c, r: w_ref[v, f, c, r : r + PAD]

    def put(v, f, c, at, value):
        part_ref[v, f, c, at] = value

    section(0.5 * time_step, parity, half, half, get, get, base_ref, tab_ref, put,
            xp_ref, None, None, None, *scratch)


def start_second(parity, half, part_ref, xp_in, xd, rp_in, rd_in, s1):
    def fill(v, f, c):
        s1[v, f, c] = part_ref[v, f, c]

    all_cells(fill)
    add_faces(parity, xp_in, xd, s1)
    add_edges(half, rp_in, rd_in, s1, [(c, c) for c in range(4)])


def own_second_kernel(w_ref, part_ref, xp_in, first_in, second_in, rp_in, rd_in, base_ref, tab_ref, _,
                      out_ref, rp_ref, rd_ref, *scratch):
    *scratch, s1 = scratch
    column, half = place()
    start_second(column, half, part_ref, xp_in, pick(z_side(), second_in, first_in), rp_in, rd_in, s1)
    get = lambda v, f, c, r: s1[v, f, c, r : r + PAD]
    start = lambda v, f, c, r: w_ref[v, f, c, r : r + PAD]

    def put(v, f, c, at, value):
        out_ref[v, f, c, at] = value

    section(time_step, column, half, half, get, start, base_ref, tab_ref, put,
            None, None, rp_ref, rd_ref, *scratch)


def partner_second_kernel(w_ref, part_ref, xp_in, first_in, second_in, message_in, part_own, xp_par, rp_own, rd_own, base_own,
                          base_ref, tab_ref, message_ref, outer_ref, xp_ref, rd_ref, *scratch):
    *scratch, s1, target, s2, xp_own = scratch
    column, half = place()

    def keep(v, f, j, at, value):
        xp_own[v, f, j, at] = value

    second_face(column, False, part_own, lambda *at: xp_par[at], rp_own, rd_own, base_own, keep, s2)
    parity = 1 - column
    rows = outer_ref.shape[3]
    n = 20 * rows
    edge = rd_ref.shape[0]
    start_second(parity, half, part_ref, xp_in, pick(z_side(), first_in, second_in), message_in.at[0:edge], message_in.at[edge : 2 * edge], s1)
    get = lambda v, f, c, r: s1[v, f, c, r : r + PAD]
    start = lambda v, f, c, r: w_ref[v, f, c, r : r + PAD]

    def put(v, f, c, at, value):
        target[v, f, c, at] = value

    section(time_step, parity, half, half, get, start, base_ref, tab_ref, put,
            xp_ref, None, message_ref.at[n : n + edge], rd_ref, *scratch)
    for v in range(2):
        for f in range(5):
            for j in range(2):
                k = ((5 * v + f) * 2 + j) * rows
                message_ref[k : k + rows] = target[v, f, 2 - 2 * parity + j] + xp_own[v, f, j]
                outer_ref[v, f, j] = target[v, f, 2 * parity + j]


def finish_kernel(outer_ref, first_in, second_in, message_ref):
    message_ref[...] = outer_ref[...] + jnp.where(z_side() == 0, first_in[...], second_in[...])


def own_last_kernel(part_ref, xp_ref, first_in, second_in, message_ref, rd_ref, out_hbm, value, sem):
    column, half = place()
    edge = rd_ref.shape[0]
    n = message_ref.shape[0] - edge
    start_second(column, half, part_ref, xp_ref, pick(z_side(), second_in, first_in), message_ref.at[n : n + edge],
                 rd_ref, value)
    copy = pltpu.make_async_copy(value, out_hbm.at[:, :, :, half], sem)
    copy.start()
    copy.wait()


def other_last_kernel(inner_ref, outer_ref, rp_ref, rd_ref, _, out_hbm, value, sem):
    column, half = place()
    rows = value.shape[3]
    for v in range(2):
        for f in range(5):
            for j in range(2):
                k = ((5 * v + f) * 2 + j) * rows
                value[v, f, 2 * column + j] = outer_ref[v, f, j]
                value[v, f, 2 - 2 * column + j] = inner_ref[k : k + rows]
    add_edges(1 - half, rp_ref, rd_ref, value, [(c, c) for c in range(4)])
    copy = pltpu.make_async_copy(value, out_hbm.at[:, :, :, 1 - half], sem)
    copy.start()
    copy.wait()


VM = pl.BlockSpec(memory_space=pltpu.VMEM)
HB = pl.BlockSpec(memory_space=pltpu.HBM)
PARAMS = pltpu.CompilerParams(vmem_limit_bytes=40 << 20)


def local(adjoint_vectors, base_density, base_velocity, base_pressure):
    vectors, fields, cells, both, width = adjoint_vectors.shape
    rows = both // 2
    if cells != 4 or vectors != 2 or rows % PAD:
        raise ValueError("unexpected block")
    f32 = jnp.float32
    shape = lambda *s: jax.ShapeDtypeStruct(s, f32)
    tab = jnp.asarray(theta_table(width))
    block, pair = shape(2, 5, cells, rows, width), shape(2, 5, 2, rows, width)
    base, edge = shape(5, cells, rows, width), shape(20 * cells, width)
    halves = lambda a: a.reshape(a.shape[:-2] + (2, rows, width))
    scratch = [
        pltpu.VMEM((2, 5, cells, rows + 2 * PAD, width), f32),
        pltpu.VMEM((2, 5, cells, rows + 2 * PAD, width), f32),
        pltpu.VMEM((2, 5, cells, rows, width), f32),
        pltpu.VMEM((10 * cells * rows, 2 * width), jnp.bfloat16),
        pltpu.VMEM((10 * cells * rows, 2 * width), jnp.bfloat16),
        pltpu.VMEM((10 * cells * rows, width), f32),
    ]
    whole = pltpu.VMEM((2, 5, cells, rows, width), f32)

    gx, row = lax.axis_size("gx"), lax.axis_size("row")
    partner = [(g, g + 1 - 2 * (g % 2)) for g in range(gx)]
    trade = lambda value: lax.ppermute(value, "gx", partner)

    def swaps(axis, apart):
        size = lax.axis_size(axis)
        found = ([], [])
        for i in range(size - apart):
            found[(i // apart) % 2].extend([(i, i + apart), (i + apart, i)])
        return found

    z_swaps, row_swaps = swaps("gx", 2), swaps("row", 1)

    def swap_both(pairs, axis, first, second):
        return lax.ppermute(first, axis, pairs[0]), lax.ppermute(second, axis, pairs[1])

    def beside(value, cross, flip):
        perm = []
        for g in range(gx):
            for j in range(row):
                side = (g + j + flip) % 2
                k = j - 1 + 2 * side
                if 0 <= k < row:
                    perm.append((g * row + j, (partner[g][1] if cross else g) * row + k))
        return lax.ppermute(value, ("gx", "row"), perm)

    def call(kernel, name, outs, ins, extra=(), **more):
        return pl.pallas_call(
            kernel, name=name, out_shape=outs, in_specs=[VM] * len(ins), out_specs=[VM] * len(outs),
            scratch_shapes=list(scratch) + list(extra), compiler_params=PARAMS, **more,
        )(*ins)

    hbm = lambda a: pltpu.with_memory_space_constraint(a, pltpu.HBM)
    small = lambda kernel, name, outs, *ins, extra=(): pl.pallas_call(
        kernel, name=name, out_shape=outs, in_specs=[VM] * len(ins),
        out_specs=[VM] * len(outs) if isinstance(outs, list) else VM, scratch_shapes=extra, compiler_params=PARAMS)(*ins)
    duo = pltpu.VMEM(pair.shape, f32)
    n, e = 20 * rows, 20 * cells
    own, other, outer, base_own, base_send, rest, table = pl.pallas_call(
        load_kernel, name="load",
        out_shape=[block, block, shape(26, rows, width), base, base, shape(34, rows, width),
                   jax.ShapeDtypeStruct(tab.shape, tab.dtype)],
        in_specs=[HB] * 5, out_specs=[VM] * 7, scratch_shapes=[pltpu.SemaphoreType.DMA((37,))],
        compiler_params=PARAMS,
    )(hbm(halves(adjoint_vectors)), hbm(halves(base_density)), hbm(halves(base_velocity)),
      hbm(halves(base_pressure)), hbm(tab))
    outer, rest = trade(outer), trade(rest)
    part_own, xp_own, xd_own, rp_own, first, rp_other, second = call(
        own_first_kernel, "own_1", [block, pair, pair, edge, edge, edge, edge],
        (own, other, base_own, base_send, table), (pltpu.VMEM(edge.shape, f32), pltpu.VMEM(edge.shape, f32)))
    message, rd_own_in = small(
        pack_kernel, "pack", [shape(2 * e, width), edge], rp_own, *swap_both(row_swaps, "row", first, second))
    faces = swap_both(z_swaps, "gx", *small(face_kernel, "face", [pair, pair], outer, xd_own, message))
    message = trade(message)
    w_par, base_par, part_par, xp_par = call(
        partner_first_kernel, "partner_1", [block, base, block, pair], (outer, rest, table))
    faces2 = swap_both(z_swaps, "gx", *small(
        outer_faces_kernel, "outer_faces", [pair, pair], part_own, part_par, *faces, rp_other, rd_own_in, message,
        base_own, base_par, extra=[duo, duo]))
    inner, outer, xp_par2, rd_par = call(
        partner_second_kernel, "partner_2", [shape(n + e, width), pair, pair, edge],
        (w_par, part_par, xp_own, *faces, message, part_own, xp_par, rp_other, rd_own_in, base_own, base_par, table),
        (whole, whole, duo, duo))
    inner = trade(inner)
    outer = small(finish_kernel, "finish", pair, outer, *faces2)
    part_own, rp_own, rd_own = call(
        own_second_kernel, "own_2", [block, edge, edge],
        (own, part_own, xp_par, *faces, rp_other, rd_own_in, base_own, table, outer), (whole,))
    outer = trade(outer)
    rd_other_in = beside(rd_par, True, 0)
    rd_own_in = beside(rd_own, False, 0)
    xp_par = xp_par2
    full = shape(2, 5, cells, 2, rows, width)
    last = dict(out_shape=full, out_specs=HB, scratch_shapes=[whole, pltpu.SemaphoreType.DMA], compiler_params=PARAMS)
    out = pl.pallas_call(own_last_kernel, name="own_3", in_specs=[VM] * 6, **last)(
        part_own, xp_par, *faces2, inner, rd_own_in)
    out = pl.pallas_call(
        other_last_kernel, name="other_3", in_specs=[VM] * 4 + [HB], input_output_aliases={4: 0}, **last,
    )(inner, outer, rp_own, rd_other_in, out)
    return out.reshape(adjoint_vectors.shape)


def solution(mesh):
    in_specs = (
        P(None, None, "gx", "row", None),
        P("gx", "row", None),
        P(None, "gx", "row", None),
        P("gx", "row", None),
    )
    out_specs = P(None, None, "gx", "row", None)
    return jax.shard_map(local, mesh=mesh, in_specs=in_specs, out_specs=out_specs, check_vma=False)
```

```python
import functools

import jax
import jax.numpy as jnp
import ml_dtypes
import numpy as np
from jax import lax
from jax.experimental import pallas as pl
from jax.experimental.pallas import tpu as pltpu
from jax.sharding import PartitionSpec as P

gamma_ratio = 1.4
viscosity = 0.1
time_step = 0.3

A1 = 8.0 / 12.0
A2 = 1.0 / 12.0
B1 = viscosity * 16.0 / 12.0
B2 = viscosity / 12.0
CENTRE = -2.0 * viscosity * 30.0 / 12.0
PAD = 8


def theta_table(azimuth):
    spacing = 2.0 * np.pi / azimuth
    index = np.arange(azimuth)
    offset = index[:, None] - index[None, :]
    signs = np.where(offset % 2 == 0, 1.0, -1.0)
    angle = offset * (spacing / 2.0)
    diagonal = offset == 0
    tangent = np.where(diagonal, 1.0, np.tan(angle))
    sine = np.where(diagonal, 1.0, np.sin(angle))
    first = np.where(diagonal, 0.0, 0.5 * signs * spacing / tangent)
    second = np.where(
        diagonal, -(np.pi**2) / 3.0 - spacing**2 / 6.0, -0.5 * signs * spacing**2 / (sine * sine)
    )
    table = np.concatenate([first.T, viscosity * second.T], axis=0).astype(np.float32)
    high = table.astype(ml_dtypes.bfloat16)
    low = (table - high.astype(np.float32)).astype(ml_dtypes.bfloat16)
    return np.concatenate([high, low], axis=1)


def fluxes(base_ref, c, at, w, directions):
    rho, pr = base_ref[0, c, at], base_ref[4, c, at]
    inv = 1.0 / rho
    pg = gamma_ratio * pr
    flows = []
    for v in range(2):
        q = rho * w[v][0] + pg * w[v][4]
        rows = []
        for d in directions:
            speed = base_ref[1 + d, c, at]
            flow = [speed * w[v][f] for f in range(5)]
            flow[1 + d] = flow[1 + d] + q
            flow[4] = flow[4] + w[v][1 + d] * inv
            rows.append(flow)
        flows.append(rows)
    return flows


def radial(fr, wp, v, f, c, r, n):
    base = PAD + r
    sh = lambda buf, k: buf[v, f, c, base + k : base + k + n]
    near = 8.0 * (sh(fr, 1) - sh(fr, -1)) - (sh(fr, 2) - sh(fr, -2))
    return near + B1 * (sh(wp, 1) + sh(wp, -1)) - B2 * (sh(wp, 2) + sh(wp, -2))


def clear_pads(fr, wp):
    _, _, cells, padded, width = fr.shape
    zeros = jnp.zeros((PAD, width), jnp.float32)
    for v in range(2):
        for f in range(5):
            for c in range(cells):
                for buf in (wp, fr):
                    buf[v, f, c, 0:PAD] = zeros
                    buf[v, f, c, padded - PAD : padded] = zeros


def put_edges(dt, line, fr, wp, rp_ref, rd_ref):
    _, _, cells, padded, _ = fr.shape
    for v in range(2):
        for f in range(5):
            for c in range(cells):
                low = dt * radial(fr, wp, v, f, c, -2, 2)
                high = dt * radial(fr, wp, v, f, c, padded - 2 * PAD, 2)
                k = 2 * ((5 * v + f) * cells + c)
                rp_ref[k : k + 2] = jnp.where(line == 0, high, low)
                rd_ref[k : k + 2] = jnp.where(line == 0, low, high)


def section(dt, parity, line, half, get, start, base_ref, tab_ref, put, xp_ref, xd_ref, rp_ref, rd_ref,
            wp, fr, fx, xh, xl, ys):
    _, cells, rows, width = base_ref.shape
    total_rows = 2 * rows * lax.axis_size("row")
    row_start = lax.axis_index("row") * (2 * rows) + half * rows
    span = 2 * cells * rows
    clear_pads(fr, wp)

    def split(flow, k, lanes):
        both = jnp.concatenate(flow, axis=0)
        high = both.astype(jnp.bfloat16)
        xh[k : k + 2 * PAD, lanes] = high
        xl[k : k + 2 * PAD, lanes] = (both - high.astype(jnp.float32)).astype(jnp.bfloat16)

    for r in range(0, rows, PAD):
        at = slice(r, r + PAD)
        inside = slice(PAD + r, 2 * PAD + r)
        index = row_start + r + lax.broadcasted_iota(jnp.int32, (PAD, width), 0)
        fac = 1.0 / (1.0 + (index.astype(jnp.float32) + 0.5) / total_rows)
        for c in range(cells):
            w = [[get(v, f, c, r) for f in range(5)] for v in range(2)]
            flows = fluxes(base_ref, c, at, w, (0, 1, 2))
            for f in range(5):
                k = f * span + (c * (rows // PAD) + r // PAD) * 2 * PAD
                for v in range(2):
                    fx[v, f, c, at] = A2 * flows[v][0][f]
                    fr[v, f, c, inside] = A2 * flows[v][1][f]
                    wp[v, f, c, inside] = w[v][f]
                split([flows[v][2][f] * fac for v in range(2)], k, slice(0, width))
                split([w[v][f] for v in range(2)], k, slice(width, 2 * width))
    both = jnp.dot(xh[...], tab_ref[...], preferred_element_type=jnp.float32)
    low = jnp.dot(xl[...], tab_ref[:, 0:width], preferred_element_type=jnp.float32)
    ys[...] = (both[:, 0:width] + both[:, width:]) + low
    for f in range(5):
        for v in range(2):
            for r in range(0, rows, PAD):
                at = slice(r, r + PAD)
                ws = [wp[v, f, c, PAD + r : 2 * PAD + r] for c in range(cells)]
                fs = [fx[v, f, c, at] for c in range(cells)]
                small = [B2 * w for w in ws]
                far_left = [a - b for a, b in zip(fs, small)]
                far_right = [-a - b for a, b in zip(fs, small)]
                large, steep = [16.0 * b for b in small], [8.0 * a for a in fs]
                left = [b - a for a, b in zip(steep, large)]
                right = [b + a for a, b in zip(steep, large)]

                def stream(i):
                    total = None
                    for k, terms in ((1, right), (-1, left), (2, far_right), (-2, far_left)):
                        if 0 <= i + k < cells:
                            total = terms[i + k] if total is None else total + terms[i + k]
                    return total

                for j in range(2 if xp_ref is not None else 0):
                    low_face = dt * stream(j - 2)
                    high_face = dt * stream(cells + j)
                    xp_ref[v, f, j, at] = jnp.where(parity == 0, high_face, low_face)
                    if xd_ref is not None:
                        xd_ref[v, f, j, at] = jnp.where(parity == 0, low_face, high_face)
                for c in range(cells):
                    k = f * span + (c * (rows // PAD) + r // PAD) * 2 * PAD + PAD * v
                    total = stream(c) + radial(fr, wp, v, f, c, r, PAD) + CENTRE * ws[c] + ys[k : k + PAD]
                    put(v, f, c, at, start(v, f, c, r) + dt * total)
    if rp_ref is not None:
        put_edges(dt, line, fr, wp, rp_ref, rd_ref)


def add_edges(line, rp_ref, rd_ref, out, cells):
    rows = out.shape[3]
    for v in range(2):
        for f in range(5):
            for c, place in cells:
                k = 2 * ((5 * v + f) * 4 + c)
                if not isinstance(c, int):
                    k = pl.multiple_of(k, 2)
                rp, rd = rp_ref[pl.ds(k, 2)], rd_ref[pl.ds(k, 2)]
                out[v, f, place, 0:2] += jnp.where(line == 0, rd, rp)
                out[v, f, place, rows - 2 : rows] += jnp.where(line == 0, rp, rd)


def add_faces(parity, xp_ref, xd, out):
    cells = out.shape[2]
    for v in range(2):
        for f in range(5):
            for j in range(2):
                out[v, f, (cells - 2) * (1 - parity) + j] += xp_ref[v, f, j]
                out[v, f, (cells - 2) * parity + j] += xd(v, f, j)


def all_cells(fn):
    for v in range(2):
        for f in range(5):
            for c in range(4):
                fn(v, f, c)


def pick(which, first_ref, second_ref):
    return lambda *at: jnp.where(which == 0, first_ref[at], second_ref[at])


def z_side():
    return (lax.axis_index("gx") // 2 + lax.axis_index("gx")) % 2


def place():
    column = lax.axis_index("gx") % 2
    return column, (column + lax.axis_index("row")) % 2


def load_kernel(w_hbm, rho_hbm, vel_hbm, pr_hbm, tab_hbm,
                own_ref, other_ref, outer_ref, base_ref, send_ref, rest_ref, tab_ref, sems):
    column, half = place()
    outer, inner = pl.ds(2 * column, 2), pl.ds(2 - 2 * column, 2)
    side = 1 - half
    pairs = []
    for v in range(2):
        for f in range(5):
            k = 2 * (5 * v + f)
            pairs.append((w_hbm.at[v, f, outer, side], outer_ref.at[k : k + 2]))
            pairs.append((w_hbm.at[v, f, inner, side], rest_ref.at[14 + k : 16 + k]))
    for ref, first, cells in ((outer_ref, 20, outer), (rest_ref, 0, inner)):
        pairs.append((rho_hbm.at[cells, side], ref.at[first : first + 2]))
        pairs.append((vel_hbm.at[0, cells, side], ref.at[first + 2 : first + 4]))
        pairs.append((pr_hbm.at[cells, side], ref.at[first + 4 : first + 6]))
    pairs.append((vel_hbm.at[1, :, side], rest_ref.at[6:10]))
    pairs.append((vel_hbm.at[2, :, side], rest_ref.at[10:14]))
    for part, ref in ((half, base_ref), (side, send_ref)):
        pairs.append((rho_hbm.at[:, part], ref.at[0]))
        pairs.append((vel_hbm.at[:, :, part], ref.at[1:4]))
        pairs.append((pr_hbm.at[:, part], ref.at[4]))
    pairs.append((w_hbm.at[:, :, :, half], own_ref))
    pairs.append((w_hbm.at[:, :, :, side], other_ref))
    pairs.append((tab_hbm, tab_ref))
    copies = [pltpu.make_async_copy(a, b, sems.at[i]) for i, (a, b) in enumerate(pairs)]
    for copy in copies:
        copy.start()
    for copy in copies:
        copy.wait()


def own_first_kernel(own_ref, other_ref, base_ref, send_ref, tab_ref,
                     part_ref, xp_ref, xd_ref, rp_ref, rd_ref, rpo_ref, rdo_ref, wp, fr, *scratch):
    *scratch, rd_own, rd_other = scratch
    column, half = place()
    _, cells, rows, _ = base_ref.shape
    get = lambda v, f, c, r: own_ref[v, f, c, r : r + PAD]

    def put(v, f, c, at, value):
        part_ref[v, f, c, at] = value

    section(0.5 * time_step, column, half, half, get, get, base_ref, tab_ref, put,
            xp_ref, xd_ref, rp_ref, rd_own, wp, fr, *scratch)
    for c in range(cells):
        for r in (0, rows - PAD):
            w = [[other_ref[v, f, c, r : r + PAD] for f in range(5)] for v in range(2)]
            flows = fluxes(send_ref, c, slice(r, r + PAD), w, (1,))
            for v in range(2):
                for f in range(5):
                    fr[v, f, c, PAD + r : 2 * PAD + r] = A2 * flows[v][0][f]
                    wp[v, f, c, PAD + r : 2 * PAD + r] = w[v][f]
    put_edges(0.5 * time_step, 1 - half, fr, wp, rpo_ref, rd_other)
    rd_ref[...] = jnp.where(column == 0, rd_other[...], rd_own[...])
    rdo_ref[...] = jnp.where(column == 0, rd_own[...], rd_other[...])


def pair_face(dt, high_side, v, w, base, put):
    flows = []
    for j in range(2):
        rho, speed, pr = base[j]
        flow = [speed * w[j][f] for f in range(5)]
        flow[1] = flow[1] + (rho * w[j][0] + gamma_ratio * pr * w[j][4])
        flow[4] = flow[4] + w[j][1] / rho
        flows.append(flow)
    for f in range(5):
        f0, f1, w0, w1 = flows[0][f], flows[1][f], w[0][f], w[1][f]
        low = (-A2 * f0 - B2 * w0, (A1 * f0 + B1 * w0) + (-A2 * f1 - B2 * w1))
        high = ((-A1 * f1 + B1 * w1) + (A2 * f0 - B2 * w0), A2 * f1 - B2 * w1)
        for j in range(2):
            put(v, f, j, dt * jnp.where(high_side, high[j], low[j]))


def face_kernel(outer_ref, own_ref, _, first_ref, second_ref):
    column, _ = place()
    rows = outer_ref.shape[1]
    for r in range(0, rows, PAD):
        at = slice(r, r + PAD)
        base = [[outer_ref[20 + 2 * i + j, at] for i in range(3)] for j in range(2)]

        def put(v, f, j, value):
            own = own_ref[v, f, j, at]
            first_ref[v, f, j, at] = jnp.where(z_side() == 0, value, own)
            second_ref[v, f, j, at] = jnp.where(z_side() == 0, own, value)

        for v in range(2):
            w = [[outer_ref[2 * (5 * v + f) + j, at] for f in range(5)] for j in range(2)]
            pair_face(0.5 * time_step, column == 0, v, w, base, put)


def second_face(parity, outer, part_ref, x_in, rp_in, rd_in, base_ref, put, s2):
    _, half = place()
    first = 2 * parity if outer else 2 - 2 * parity
    rows = part_ref.shape[3]
    for v in range(2):
        for f in range(5):
            for j in range(2):
                s2[v, f, j] = part_ref[v, f, first + j] + x_in(v, f, j)
    add_edges(half, rp_in, rd_in, s2, [(first + j, j) for j in range(2)])
    for r in range(0, rows, PAD):
        at = slice(r, r + PAD)
        base = [[base_ref[i, first + j, at] for i in (0, 1, 4)] for j in range(2)]
        for v in range(2):
            w = [[s2[v, f, j, at] for f in range(5)] for j in range(2)]
            pair_face(time_step, (parity == 1) if outer else (parity == 0), v, w, base,
                      lambda v, f, j, value: put(v, f, j, at, value))


def outer_faces_kernel(part_own, part_par, first_in, second_in, rp_own, rd_own, message_in, base_own, base_par,
                       first_ref, second_ref, s2, face):
    column, _ = place()
    side = z_side()
    edge = rp_own.shape[0]

    def keep(v, f, j, at, value):
        face[v, f, j, at] = value

    def put(v, f, j, at, value):
        own = face[v, f, j, at]
        first_ref[v, f, j, at] = jnp.where(side == 0, value, own)
        second_ref[v, f, j, at] = jnp.where(side == 0, own, value)

    second_face(column, True, part_own, pick(side, second_in, first_in), rp_own, rd_own, base_own, keep, s2)
    second_face(1 - column, True, part_par, pick(side, first_in, second_in), message_in.at[0:edge],
                message_in.at[edge : 2 * edge], base_par, put, s2)


def pack_kernel(rp_ref, first_ref, second_ref, message_ref, rd_ref):
    column, _ = place()
    edge = rp_ref.shape[0]
    message_ref[0:edge] = rp_ref[...]
    message_ref[edge : 2 * edge] = jnp.where(column == 0, first_ref[...], second_ref[...])
    rd_ref[...] = jnp.where(column == 0, second_ref[...], first_ref[...])


def partner_first_kernel(outer_ref, rest_ref, tab_ref, w_ref, base_ref, part_ref, xp_ref, *scratch):
    column, half = place()
    parity = 1 - column
    first, second = 2 * parity, 2 - 2 * parity
    for j in range(2):
        for v in range(2):
            for f in range(5):
                k = 2 * (5 * v + f) + j
                w_ref[v, f, first + j] = outer_ref[k]
                w_ref[v, f, second + j] = rest_ref[14 + k]
        for i, field in enumerate((0, 1, 4)):
            base_ref[field, first + j] = outer_ref[20 + 2 * i + j]
            base_ref[field, second + j] = rest_ref[2 * i + j]
    for c in range(4):
        base_ref[2, c] = rest_ref[6 + c]
        base_ref[3, c] = rest_ref[10 + c]
    get = lambda v, f, c, r: w_ref[v, f, c, r : r + PAD]

    def put(v, f, c, at, value):
        part_ref[v, f, c, at] = value

    section(0.5 * time_step, parity, half, half, get, get, base_ref, tab_ref, put,
            xp_ref, None, None, None, *scratch)


def start_second(parity, half, part_ref, xp_in, xd, rp_in, rd_in, s1):
    def fill(v, f, c):
        s1[v, f, c] = part_ref[v, f, c]

    all_cells(fill)
    add_faces(parity, xp_in, xd, s1)
    add_edges(half, rp_in, rd_in, s1, [(c, c) for c in range(4)])


def own_second_kernel(w_ref, part_ref, xp_in, first_in, second_in, rp_in, rd_in, base_ref, tab_ref, _,
                      out_ref, rp_ref, rd_ref, *scratch):
    *scratch, s1 = scratch
    column, half = place()
    start_second(column, half, part_ref, xp_in, pick(z_side(), second_in, first_in), rp_in, rd_in, s1)
    get = lambda v, f, c, r: s1[v, f, c, r : r + PAD]
    start = lambda v, f, c, r: w_ref[v, f, c, r : r + PAD]

    def put(v, f, c, at, value):
        out_ref[v, f, c, at] = value

    section(time_step, column, half, half, get, start, base_ref, tab_ref, put,
            None, None, rp_ref, rd_ref, *scratch)


def partner_second_kernel(w_ref, part_ref, xp_in, first_in, second_in, message_in, part_own, xp_par, rp_own, rd_own, base_own,
                          base_ref, tab_ref, message_ref, outer_ref, xp_ref, rd_ref, *scratch):
    *scratch, s1, target, s2, xp_own = scratch
    column, half = place()

    def keep(v, f, j, at, value):
        xp_own[v, f, j, at] = value

    second_face(column, False, part_own, lambda *at: xp_par[at], rp_own, rd_own, base_own, keep, s2)
    parity = 1 - column
    rows = outer_ref.shape[3]
    n = 20 * rows
    edge = rd_ref.shape[0]
    start_second(parity, half, part_ref, xp_in, pick(z_side(), first_in, second_in), message_in.at[0:edge], message_in.at[edge : 2 * edge], s1)
    get = lambda v, f, c, r: s1[v, f, c, r : r + PAD]
    start = lambda v, f, c, r: w_ref[v, f, c, r : r + PAD]

    def put(v, f, c, at, value):
        target[v, f, c, at] = value

    section(time_step, parity, half, half, get, start, base_ref, tab_ref, put,
            xp_ref, None, message_ref.at[n : n + edge], rd_ref, *scratch)
    for v in range(2):
        for f in range(5):
            for j in range(2):
                k = ((5 * v + f) * 2 + j) * rows
                message_ref[k : k + rows] = target[v, f, 2 - 2 * parity + j] + xp_own[v, f, j]
                outer_ref[v, f, j] = target[v, f, 2 * parity + j]


def finish_kernel(outer_ref, first_in, second_in, _, message_ref):
    message_ref[...] = outer_ref[...] + jnp.where(z_side() == 0, first_in[...], second_in[...])


def own_last_kernel(part_ref, xp_ref, first_in, second_in, message_ref, rd_ref, out_hbm, value, sem):
    column, half = place()
    edge = rd_ref.shape[0]
    n = message_ref.shape[0] - edge
    start_second(column, half, part_ref, xp_ref, pick(z_side(), second_in, first_in), message_ref.at[n : n + edge],
                 rd_ref, value)
    copy = pltpu.make_async_copy(value, out_hbm.at[:, :, :, half], sem)
    copy.start()
    copy.wait()


def other_last_kernel(inner_ref, outer_ref, rp_ref, rd_ref, _, out_hbm, value, sem):
    column, half = place()
    rows = value.shape[3]
    for v in range(2):
        for f in range(5):
            for j in range(2):
                k = ((5 * v + f) * 2 + j) * rows
                value[v, f, 2 * column + j] = outer_ref[v, f, j]
                value[v, f, 2 - 2 * column + j] = inner_ref[k : k + rows]
    add_edges(1 - half, rp_ref, rd_ref, value, [(c, c) for c in range(4)])
    copy = pltpu.make_async_copy(value, out_hbm.at[:, :, :, 1 - half], sem)
    copy.start()
    copy.wait()


VM = pl.BlockSpec(memory_space=pltpu.VMEM)
HB = pl.BlockSpec(memory_space=pltpu.HBM)
PARAMS = pltpu.CompilerParams(vmem_limit_bytes=40 << 20)


def local(adjoint_vectors, base_density, base_velocity, base_pressure):
    vectors, fields, cells, both, width = adjoint_vectors.shape
    rows = both // 2
    if cells != 4 or vectors != 2 or rows % PAD:
        raise ValueError("unexpected block")
    f32 = jnp.float32
    shape = lambda *s: jax.ShapeDtypeStruct(s, f32)
    tab = jnp.asarray(theta_table(width))
    block, pair = shape(2, 5, cells, rows, width), shape(2, 5, 2, rows, width)
    base, edge = shape(5, cells, rows, width), shape(20 * cells, width)
    halves = lambda a: a.reshape(a.shape[:-2] + (2, rows, width))
    scratch = [
        pltpu.VMEM((2, 5, cells, rows + 2 * PAD, width), f32),
        pltpu.VMEM((2, 5, cells, rows + 2 * PAD, width), f32),
        pltpu.VMEM((2, 5, cells, rows, width), f32),
        pltpu.VMEM((10 * cells * rows, 2 * width), jnp.bfloat16),
        pltpu.VMEM((10 * cells * rows, 2 * width), jnp.bfloat16),
        pltpu.VMEM((10 * cells * rows, width), f32),
    ]
    whole = pltpu.VMEM((2, 5, cells, rows, width), f32)

    gx, row = lax.axis_size("gx"), lax.axis_size("row")
    partner = [(g, g + 1 - 2 * (g % 2)) for g in range(gx)]
    trade = lambda value: lax.ppermute(value, "gx", partner)

    def swaps(axis, apart):
        size = lax.axis_size(axis)
        found = ([], [])
        for i in range(size - apart):
            found[(i // apart) % 2].extend([(i, i + apart), (i + apart, i)])
        return found

    z_swaps, row_swaps = swaps("gx", 2), swaps("row", 1)

    def swap_both(pairs, axis, first, second):
        return lax.ppermute(first, axis, pairs[0]), lax.ppermute(second, axis, pairs[1])

    def beside(value, cross, flip):
        perm = []
        for g in range(gx):
            for j in range(row):
                side = (g + j + flip) % 2
                k = j - 1 + 2 * side
                if 0 <= k < row:
                    perm.append((g * row + j, (partner[g][1] if cross else g) * row + k))
        return lax.ppermute(value, ("gx", "row"), perm)

    def call(kernel, name, outs, ins, extra=(), **more):
        return pl.pallas_call(
            kernel, name=name, out_shape=outs, in_specs=[VM] * len(ins), out_specs=[VM] * len(outs),
            scratch_shapes=list(scratch) + list(extra), compiler_params=PARAMS, **more,
        )(*ins)

    hbm = lambda a: pltpu.with_memory_space_constraint(a, pltpu.HBM)
    small = lambda kernel, name, outs, *ins, extra=(): pl.pallas_call(
        kernel, name=name, out_shape=outs, in_specs=[VM] * len(ins),
        out_specs=[VM] * len(outs) if isinstance(outs, list) else VM, scratch_shapes=extra, compiler_params=PARAMS)(*ins)
    duo = pltpu.VMEM(pair.shape, f32)
    n, e = 20 * rows, 20 * cells
    own, other, outer, base_own, base_send, rest, table = pl.pallas_call(
        load_kernel, name="load",
        out_shape=[block, block, shape(26, rows, width), base, base, shape(34, rows, width),
                   jax.ShapeDtypeStruct(tab.shape, tab.dtype)],
        in_specs=[HB] * 5, out_specs=[VM] * 7, scratch_shapes=[pltpu.SemaphoreType.DMA((37,))],
        compiler_params=PARAMS,
    )(hbm(halves(adjoint_vectors)), hbm(halves(base_density)), hbm(halves(base_velocity)),
      hbm(halves(base_pressure)), hbm(tab))
    outer, rest = trade(outer), trade(rest)
    part_own, xp_own, xd_own, rp_own, first, rp_other, second = call(
        own_first_kernel, "own_1", [block, pair, pair, edge, edge, edge, edge],
        (own, other, base_own, base_send, table), (pltpu.VMEM(edge.shape, f32), pltpu.VMEM(edge.shape, f32)))
    message, rd_own_in = small(
        pack_kernel, "pack", [shape(2 * e, width), edge], rp_own, *swap_both(row_swaps, "row", first, second))
    faces = swap_both(z_swaps, "gx", *small(face_kernel, "face", [pair, pair], outer, xd_own, message))
    message = trade(message)
    w_par, base_par, part_par, xp_par = call(
        partner_first_kernel, "partner_1", [block, base, block, pair], (outer, rest, table))
    faces2 = swap_both(z_swaps, "gx", *small(
        outer_faces_kernel, "outer_faces", [pair, pair], part_own, part_par, *faces, rp_other, rd_own_in, message,
        base_own, base_par, extra=[duo, duo]))
    inner, outer, xp_par2, rd_par = call(
        partner_second_kernel, "partner_2", [shape(n + e, width), pair, pair, edge],
        (w_par, part_par, xp_own, *faces, message, part_own, xp_par, rp_other, rd_own_in, base_own, base_par, table),
        (whole, whole, duo, duo))
    inner = trade(inner)
    part_own, rp_own, rd_own = call(
        own_second_kernel, "own_2", [block, edge, edge],
        (own, part_own, xp_par, *faces, rp_other, rd_own_in, base_own, table, rd_par), (whole,))
    outer = small(finish_kernel, "finish", pair, outer, *faces2, rd_own)
    outer = trade(outer)
    rd_other_in = beside(rd_par, True, 0)
    rd_own_in = beside(rd_own, False, 0)
    xp_par = xp_par2
    full = shape(2, 5, cells, 2, rows, width)
    last = dict(out_shape=full, out_specs=HB, scratch_shapes=[whole, pltpu.SemaphoreType.DMA], compiler_params=PARAMS)
    out = pl.pallas_call(own_last_kernel, name="own_3", in_specs=[VM] * 6, **last)(
        part_own, xp_par, *faces2, inner, rd_own_in)
    out = pl.pallas_call(
        other_last_kernel, name="other_3", in_specs=[VM] * 4 + [HB], input_output_aliases={4: 0}, **last,
    )(inner, outer, rp_own, rd_other_in, out)
    return out.reshape(adjoint_vectors.shape)


def solution(mesh):
    in_specs = (
        P(None, None, "gx", "row", None),
        P("gx", "row", None),
        P(None, "gx", "row", None),
        P("gx", "row", None),
    )
    out_specs = P(None, None, "gx", "row", None)
    return jax.shard_map(local, mesh=mesh, in_specs=in_specs, out_specs=out_specs, check_vma=False)
```

```python
import functools

import jax
import jax.numpy as jnp
import ml_dtypes
import numpy as np
from jax import lax
from jax.experimental import pallas as pl
from jax.experimental.pallas import tpu as pltpu
from jax.sharding import PartitionSpec as P

gamma_ratio = 1.4
viscosity = 0.1
time_step = 0.3

A1 = 8.0 / 12.0
A2 = 1.0 / 12.0
B1 = viscosity * 16.0 / 12.0
B2 = viscosity / 12.0
CENTRE = -2.0 * viscosity * 30.0 / 12.0
PAD = 8


def theta_table(azimuth):
    spacing = 2.0 * np.pi / azimuth
    index = np.arange(azimuth)
    offset = index[:, None] - index[None, :]
    signs = np.where(offset % 2 == 0, 1.0, -1.0)
    angle = offset * (spacing / 2.0)
    diagonal = offset == 0
    tangent = np.where(diagonal, 1.0, np.tan(angle))
    sine = np.where(diagonal, 1.0, np.sin(angle))
    first = np.where(diagonal, 0.0, 0.5 * signs * spacing / tangent)
    second = np.where(
        diagonal, -(np.pi**2) / 3.0 - spacing**2 / 6.0, -0.5 * signs * spacing**2 / (sine * sine)
    )
    table = np.concatenate([first.T, viscosity * second.T], axis=0).astype(np.float32)
    high = table.astype(ml_dtypes.bfloat16)
    low = (table - high.astype(np.float32)).astype(ml_dtypes.bfloat16)
    return np.concatenate([high, low], axis=1)


def fluxes(base_ref, c, at, w, directions):
    rho, pr = base_ref[0, c, at], base_ref[4, c, at]
    inv = 1.0 / rho
    pg = gamma_ratio * pr
    flows = []
    for v in range(2):
        q = rho * w[v][0] + pg * w[v][4]
        rows = []
        for d in directions:
            speed = base_ref[1 + d, c, at]
            flow = [speed * w[v][f] for f in range(5)]
            flow[1 + d] = flow[1 + d] + q
            flow[4] = flow[4] + w[v][1 + d] * inv
            rows.append(flow)
        flows.append(rows)
    return flows


def radial(fr, wp, v, f, c, r, n):
    base = PAD + r
    sh = lambda buf, k: buf[v, f, c, base + k : base + k + n]
    near = 8.0 * (sh(fr, 1) - sh(fr, -1)) - (sh(fr, 2) - sh(fr, -2))
    return near + B1 * (sh(wp, 1) + sh(wp, -1)) - B2 * (sh(wp, 2) + sh(wp, -2))


def clear_pads(fr, wp):
    _, _, cells, padded, width = fr.shape
    zeros = jnp.zeros((PAD, width), jnp.float32)
    for v in range(2):
        for f in range(5):
            for c in range(cells):
                for buf in (wp, fr):
                    buf[v, f, c, 0:PAD] = zeros
                    buf[v, f, c, padded - PAD : padded] = zeros


def put_edges(dt, line, fr, wp, rp_ref, rd_ref):
    _, _, cells, padded, _ = fr.shape
    for v in range(2):
        for f in range(5):
            for c in range(cells):
                low = dt * radial(fr, wp, v, f, c, -2, 2)
                high = dt * radial(fr, wp, v, f, c, padded - 2 * PAD, 2)
                k = 2 * ((5 * v + f) * cells + c)
                rp_ref[k : k + 2] = jnp.where(line == 0, high, low)
                rd_ref[k : k + 2] = jnp.where(line == 0, low, high)


def section(dt, parity, line, half, get, start, base_ref, tab_ref, put, xp_ref, xd_ref, rp_ref, rd_ref,
            wp, fr, fx, xh, xl, ys):
    _, cells, rows, width = base_ref.shape
    total_rows = 2 * rows * lax.axis_size("row")
    row_start = lax.axis_index("row") * (2 * rows) + half * rows
    span = 2 * cells * rows
    clear_pads(fr, wp)

    def split(flow, k, lanes):
        both = jnp.concatenate(flow, axis=0)
        high = both.astype(jnp.bfloat16)
        xh[k : k + 2 * PAD, lanes] = high
        xl[k : k + 2 * PAD, lanes] = (both - high.astype(jnp.float32)).astype(jnp.bfloat16)

    for r in range(0, rows, PAD):
        at = slice(r, r + PAD)
        inside = slice(PAD + r, 2 * PAD + r)
        index = row_start + r + lax.broadcasted_iota(jnp.int32, (PAD, width), 0)
        fac = 1.0 / (1.0 + (index.astype(jnp.float32) + 0.5) / total_rows)
        for c in range(cells):
            w = [[get(v, f, c, r) for f in range(5)] for v in range(2)]
            flows = fluxes(base_ref, c, at, w, (0, 1, 2))
            for f in range(5):
                k = f * span + (c * (rows // PAD) + r // PAD) * 2 * PAD
                for v in range(2):
                    fx[v, f, c, at] = A2 * flows[v][0][f]
                    fr[v, f, c, inside] = A2 * flows[v][1][f]
                    wp[v, f, c, inside] = w[v][f]
                split([flows[v][2][f] * fac for v in range(2)], k, slice(0, width))
                split([w[v][f] for v in range(2)], k, slice(width, 2 * width))
    both = jnp.dot(xh[...], tab_ref[...], preferred_element_type=jnp.float32)
    low = jnp.dot(xl[...], tab_ref[:, 0:width], preferred_element_type=jnp.float32)
    ys[...] = (both[:, 0:width] + both[:, width:]) + low
    for f in range(5):
        for v in range(2):
            for r in range(0, rows, PAD):
                at = slice(r, r + PAD)
                ws = [wp[v, f, c, PAD + r : 2 * PAD + r] for c in range(cells)]
                fs = [fx[v, f, c, at] for c in range(cells)]
                small = [B2 * w for w in ws]
                far_left = [a - b for a, b in zip(fs, small)]
                far_right = [-a - b for a, b in zip(fs, small)]
                large, steep = [16.0 * b for b in small], [8.0 * a for a in fs]
                left = [b - a for a, b in zip(steep, large)]
                right = [b + a for a, b in zip(steep, large)]

                def stream(i):
                    total = None
                    for k, terms in ((1, right), (-1, left), (2, far_right), (-2, far_left)):
                        if 0 <= i + k < cells:
                            total = terms[i + k] if total is None else total + terms[i + k]
                    return total

                for j in range(2 if xp_ref is not None else 0):
                    low_face = dt * stream(j - 2)
                    high_face = dt * stream(cells + j)
                    xp_ref[v, f, j, at] = jnp.where(parity == 0, high_face, low_face)
                    if xd_ref is not None:
                        xd_ref[v, f, j, at] = jnp.where(parity == 0, low_face, high_face)
                for c in range(cells):
                    k = f * span + (c * (rows // PAD) + r // PAD) * 2 * PAD + PAD * v
                    total = stream(c) + radial(fr, wp, v, f, c, r, PAD) + CENTRE * ws[c] + ys[k : k + PAD]
                    put(v, f, c, at, start(v, f, c, r) + dt * total)
    if rp_ref is not None:
        put_edges(dt, line, fr, wp, rp_ref, rd_ref)


def add_edges(line, rp_ref, rd_ref, out, cells):
    rows = out.shape[3]
    for v in range(2):
        for f in range(5):
            for c, place in cells:
                k = 2 * ((5 * v + f) * 4 + c)
                if not isinstance(c, int):
                    k = pl.multiple_of(k, 2)
                rp, rd = rp_ref[pl.ds(k, 2)], rd_ref[pl.ds(k, 2)]
                out[v, f, place, 0:2] += jnp.where(line == 0, rd, rp)
                out[v, f, place, rows - 2 : rows] += jnp.where(line == 0, rp, rd)


def add_faces(parity, xp_ref, xd, out):
    cells = out.shape[2]
    for v in range(2):
        for f in range(5):
            for j in range(2):
                out[v, f, (cells - 2) * (1 - parity) + j] += xp_ref[v, f, j]
                out[v, f, (cells - 2) * parity + j] += xd(v, f, j)


def all_cells(fn):
    for v in range(2):
        for f in range(5):
            for c in range(4):
                fn(v, f, c)


def pick(which, first_ref, second_ref):
    return lambda *at: jnp.where(which == 0, first_ref[at], second_ref[at])


def z_side():
    return (lax.axis_index("gx") // 2 + lax.axis_index("gx")) % 2


def place():
    column = lax.axis_index("gx") % 2
    return column, (column + lax.axis_index("row")) % 2


def load_kernel(w_hbm, rho_hbm, vel_hbm, pr_hbm, tab_hbm,
                own_ref, other_ref, outer_ref, base_ref, send_ref, rest_ref, tab_ref, sems):
    column, half = place()
    outer, inner = pl.ds(2 * column, 2), pl.ds(2 - 2 * column, 2)
    side = 1 - half
    pairs = []
    for v in range(2):
        for f in range(5):
            k = 2 * (5 * v + f)
            pairs.append((w_hbm.at[v, f, outer, side], outer_ref.at[k : k + 2]))
            pairs.append((w_hbm.at[v, f, inner, side], rest_ref.at[14 + k : 16 + k]))
    for ref, first, cells in ((outer_ref, 20, outer), (rest_ref, 0, inner)):
        pairs.append((rho_hbm.at[cells, side], ref.at[first : first + 2]))
        pairs.append((vel_hbm.at[0, cells, side], ref.at[first + 2 : first + 4]))
        pairs.append((pr_hbm.at[cells, side], ref.at[first + 4 : first + 6]))
    pairs.append((vel_hbm.at[1, :, side], rest_ref.at[6:10]))
    pairs.append((vel_hbm.at[2, :, side], rest_ref.at[10:14]))
    for part, ref in ((half, base_ref), (side, send_ref)):
        pairs.append((rho_hbm.at[:, part], ref.at[0]))
        pairs.append((vel_hbm.at[:, :, part], ref.at[1:4]))
        pairs.append((pr_hbm.at[:, part], ref.at[4]))
    pairs.append((w_hbm.at[:, :, :, half], own_ref))
    pairs.append((w_hbm.at[:, :, :, side], other_ref))
    pairs.append((tab_hbm, tab_ref))
    copies = [pltpu.make_async_copy(a, b, sems.at[i]) for i, (a, b) in enumerate(pairs)]
    for copy in copies:
        copy.start()
    for copy in copies:
        copy.wait()


def own_first_kernel(own_ref, other_ref, base_ref, send_ref, tab_ref,
                     part_ref, xp_ref, xd_ref, rp_ref, rd_ref, rpo_ref, rdo_ref, wp, fr, *scratch):
    *scratch, rd_own, rd_other = scratch
    column, half = place()
    _, cells, rows, _ = base_ref.shape
    get = lambda v, f, c, r: own_ref[v, f, c, r : r + PAD]

    def put(v, f, c, at, value):
        part_ref[v, f, c, at] = value

    section(0.5 * time_step, column, half, half, get, get, base_ref, tab_ref, put,
            xp_ref, xd_ref, rp_ref, rd_own, wp, fr, *scratch)
    for c in range(cells):
        for r in (0, rows - PAD):
            w = [[other_ref[v, f, c, r : r + PAD] for f in range(5)] for v in range(2)]
            flows = fluxes(send_ref, c, slice(r, r + PAD), w, (1,))
            for v in range(2):
                for f in range(5):
                    fr[v, f, c, PAD + r : 2 * PAD + r] = A2 * flows[v][0][f]
                    wp[v, f, c, PAD + r : 2 * PAD + r] = w[v][f]
    put_edges(0.5 * time_step, 1 - half, fr, wp, rpo_ref, rd_other)
    rd_ref[...] = jnp.where(column == 0, rd_other[...], rd_own[...])
    rdo_ref[...] = jnp.where(column == 0, rd_own[...], rd_other[...])


def pair_face(dt, high_side, v, w, base, put):
    flows = []
    for j in range(2):
        rho, speed, pr = base[j]
        flow = [speed * w[j][f] for f in range(5)]
        flow[1] = flow[1] + (rho * w[j][0] + gamma_ratio * pr * w[j][4])
        flow[4] = flow[4] + w[j][1] / rho
        flows.append(flow)
    for f in range(5):
        f0, f1, w0, w1 = flows[0][f], flows[1][f], w[0][f], w[1][f]
        low = (-A2 * f0 - B2 * w0, (A1 * f0 + B1 * w0) + (-A2 * f1 - B2 * w1))
        high = ((-A1 * f1 + B1 * w1) + (A2 * f0 - B2 * w0), A2 * f1 - B2 * w1)
        for j in range(2):
            put(v, f, j, dt * jnp.where(high_side, high[j], low[j]))


def face_kernel(outer_ref, own_ref, _, first_ref, second_ref):
    column, _ = place()
    rows = outer_ref.shape[1]
    for r in range(0, rows, PAD):
        at = slice(r, r + PAD)
        base = [[outer_ref[20 + 2 * i + j, at] for i in range(3)] for j in range(2)]

        def put(v, f, j, value):
            own = own_ref[v, f, j, at]
            first_ref[v, f, j, at] = jnp.where(z_side() == 0, value, own)
            second_ref[v, f, j, at] = jnp.where(z_side() == 0, own, value)

        for v in range(2):
            w = [[outer_ref[2 * (5 * v + f) + j, at] for f in range(5)] for j in range(2)]
            pair_face(0.5 * time_step, column == 0, v, w, base, put)


def second_face(parity, outer, part_ref, x_in, rp_in, rd_in, base_ref, put, s2):
    _, half = place()
    first = 2 * parity if outer else 2 - 2 * parity
    rows = part_ref.shape[3]
    for v in range(2):
        for f in range(5):
            for j in range(2):
                s2[v, f, j] = part_ref[v, f, first + j] + x_in(v, f, j)
    add_edges(half, rp_in, rd_in, s2, [(first + j, j) for j in range(2)])
    for r in range(0, rows, PAD):
        at = slice(r, r + PAD)
        base = [[base_ref[i, first + j, at] for i in (0, 1, 4)] for j in range(2)]
        for v in range(2):
            w = [[s2[v, f, j, at] for f in range(5)] for j in range(2)]
            pair_face(time_step, (parity == 1) if outer else (parity == 0), v, w, base,
                      lambda v, f, j, value: put(v, f, j, at, value))


def outer_faces_kernel(part_own, part_par, first_in, second_in, rp_own, rd_own, message_in, base_own, base_par,
                       first_ref, second_ref, s2, face):
    column, _ = place()
    side = z_side()
    edge = rp_own.shape[0]

    def keep(v, f, j, at, value):
        face[v, f, j, at] = value

    def put(v, f, j, at, value):
        own = face[v, f, j, at]
        first_ref[v, f, j, at] = jnp.where(side == 0, value, own)
        second_ref[v, f, j, at] = jnp.where(side == 0, own, value)

    second_face(column, True, part_own, pick(side, second_in, first_in), rp_own, rd_own, base_own, keep, s2)
    second_face(1 - column, True, part_par, pick(side, first_in, second_in), message_in.at[0:edge],
                message_in.at[edge : 2 * edge], base_par, put, s2)


def pack_kernel(rp_ref, first_ref, second_ref, message_ref, rd_ref):
    column, _ = place()
    edge = rp_ref.shape[0]
    message_ref[0:edge] = rp_ref[...]
    message_ref[edge : 2 * edge] = jnp.where(column == 0, first_ref[...], second_ref[...])
    rd_ref[...] = jnp.where(column == 0, second_ref[...], first_ref[...])


def partner_first_kernel(outer_ref, rest_ref, tab_ref, w_ref, base_ref, part_ref, xp_ref, *scratch):
    column, half = place()
    parity = 1 - column
    first, second = 2 * parity, 2 - 2 * parity
    for j in range(2):
        for v in range(2):
            for f in range(5):
                k = 2 * (5 * v + f) + j
                w_ref[v, f, first + j] = outer_ref[k]
                w_ref[v, f, second + j] = rest_ref[14 + k]
        for i, field in enumerate((0, 1, 4)):
            base_ref[field, first + j] = outer_ref[20 + 2 * i + j]
            base_ref[field, second + j] = rest_ref[2 * i + j]
    for c in range(4):
        base_ref[2, c] = rest_ref[6 + c]
        base_ref[3, c] = rest_ref[10 + c]
    get = lambda v, f, c, r: w_ref[v, f, c, r : r + PAD]

    def put(v, f, c, at, value):
        part_ref[v, f, c, at] = value

    section(0.5 * time_step, parity, half, half, get, get, base_ref, tab_ref, put,
            xp_ref, None, None, None, *scratch)


def start_second(parity, half, part_ref, xp_in, xd, rp_in, rd_in, s1):
    def fill(v, f, c):
        s1[v, f, c] = part_ref[v, f, c]

    all_cells(fill)
    add_faces(parity, xp_in, xd, s1)
    add_edges(half, rp_in, rd_in, s1, [(c, c) for c in range(4)])


def own_second_kernel(w_ref, part_ref, xp_in, first_in, second_in, rp_in, rd_in, base_ref, tab_ref, _,
                      out_ref, rp_ref, rd_ref, *scratch):
    *scratch, s1 = scratch
    column, half = place()
    start_second(column, half, part_ref, xp_in, pick(z_side(), second_in, first_in), rp_in, rd_in, s1)
    get = lambda v, f, c, r: s1[v, f, c, r : r + PAD]
    start = lambda v, f, c, r: w_ref[v, f, c, r : r + PAD]

    def put(v, f, c, at, value):
        out_ref[v, f, c, at] = value

    section(time_step, column, half, half, get, start, base_ref, tab_ref, put,
            None, None, rp_ref, rd_ref, *scratch)


def partner_second_kernel(w_ref, part_ref, xp_in, first_in, second_in, message_in, part_own, xp_par, rp_own, rd_own, base_own,
                          base_ref, tab_ref, message_ref, outer_ref, xp_ref, rd_ref, *scratch):
    *scratch, s1, target, s2, xp_own = scratch
    column, half = place()

    def keep(v, f, j, at, value):
        xp_own[v, f, j, at] = value

    second_face(column, False, part_own, lambda *at: xp_par[at], rp_own, rd_own, base_own, keep, s2)
    parity = 1 - column
    rows = outer_ref.shape[3]
    n = 20 * rows
    edge = rd_ref.shape[0]
    start_second(parity, half, part_ref, xp_in, pick(z_side(), first_in, second_in), message_in.at[0:edge], message_in.at[edge : 2 * edge], s1)
    get = lambda v, f, c, r: s1[v, f, c, r : r + PAD]
    start = lambda v, f, c, r: w_ref[v, f, c, r : r + PAD]

    def put(v, f, c, at, value):
        target[v, f, c, at] = value

    section(time_step, parity, half, half, get, start, base_ref, tab_ref, put,
            xp_ref, None, message_ref.at[n : n + edge], rd_ref, *scratch)
    for v in range(2):
        for f in range(5):
            for j in range(2):
                k = ((5 * v + f) * 2 + j) * rows
                message_ref[k : k + rows] = target[v, f, 2 - 2 * parity + j] + xp_own[v, f, j]
                outer_ref[v, f, j] = target[v, f, 2 * parity + j]


def finish_kernel(outer_ref, first_in, second_in, _, message_ref):
    message_ref[...] = outer_ref[...] + jnp.where(z_side() == 0, first_in[...], second_in[...])


def own_last_kernel(part_ref, xp_ref, first_in, second_in, message_ref, rd_ref, out_hbm, value, sem):
    column, half = place()
    edge = rd_ref.shape[0]
    n = message_ref.shape[0] - edge
    start_second(column, half, part_ref, xp_ref, pick(z_side(), second_in, first_in), message_ref.at[n : n + edge],
                 rd_ref, value)
    copy = pltpu.make_async_copy(value, out_hbm.at[:, :, :, half], sem)
    copy.start()
    copy.wait()


def other_last_kernel(inner_ref, outer_ref, rp_ref, rd_ref, _, out_hbm, value, sems):
    column, half = place()
    side = 1 - half
    rows = value.shape[3]
    copies = []
    for v in range(2):
        for f in range(5):
            for j in range(2):
                k = ((5 * v + f) * 2 + j) * rows
                value[v, f, 2 * column + j] = outer_ref[v, f, j]
                value[v, f, 2 - 2 * column + j] = inner_ref[k : k + rows]
            for c in range(4):
                k = 2 * ((5 * v + f) * 4 + c)
                rp, rd = rp_ref[k : k + 2], rd_ref[k : k + 2]
                value[v, f, c, 0:2] += jnp.where(side == 0, rd, rp)
                value[v, f, c, rows - 2 : rows] += jnp.where(side == 0, rp, rd)
        copies.append(pltpu.make_async_copy(value.at[v], out_hbm.at[v, :, :, side], sems.at[v]))
        copies[v].start()
    for copy in copies:
        copy.wait()


VM = pl.BlockSpec(memory_space=pltpu.VMEM)
HB = pl.BlockSpec(memory_space=pltpu.HBM)
PARAMS = pltpu.CompilerParams(vmem_limit_bytes=40 << 20)


def local(adjoint_vectors, base_density, base_velocity, base_pressure):
    vectors, fields, cells, both, width = adjoint_vectors.shape
    rows = both // 2
    if cells != 4 or vectors != 2 or rows % PAD:
        raise ValueError("unexpected block")
    f32 = jnp.float32
    shape = lambda *s: jax.ShapeDtypeStruct(s, f32)
    tab = jnp.asarray(theta_table(width))
    block, pair = shape(2, 5, cells, rows, width), shape(2, 5, 2, rows, width)
    base, edge = shape(5, cells, rows, width), shape(20 * cells, width)
    halves = lambda a: a.reshape(a.shape[:-2] + (2, rows, width))
    scratch = [
        pltpu.VMEM((2, 5, cells, rows + 2 * PAD, width), f32),
        pltpu.VMEM((2, 5, cells, rows + 2 * PAD, width), f32),
        pltpu.VMEM((2, 5, cells, rows, width), f32),
        pltpu.VMEM((10 * cells * rows, 2 * width), jnp.bfloat16),
        pltpu.VMEM((10 * cells * rows, 2 * width), jnp.bfloat16),
        pltpu.VMEM((10 * cells * rows, width), f32),
    ]
    whole = pltpu.VMEM((2, 5, cells, rows, width), f32)

    gx, row = lax.axis_size("gx"), lax.axis_size("row")
    partner = [(g, g + 1 - 2 * (g % 2)) for g in range(gx)]
    trade = lambda value: lax.ppermute(value, "gx", partner)

    def swaps(axis, apart):
        size = lax.axis_size(axis)
        found = ([], [])
        for i in range(size - apart):
            found[(i // apart) % 2].extend([(i, i + apart), (i + apart, i)])
        return found

    z_swaps, row_swaps = swaps("gx", 2), swaps("row", 1)

    def swap_both(pairs, axis, first, second):
        return lax.ppermute(first, axis, pairs[0]), lax.ppermute(second, axis, pairs[1])

    def beside(value, cross, flip):
        perm = []
        for g in range(gx):
            for j in range(row):
                side = (g + j + flip) % 2
                k = j - 1 + 2 * side
                if 0 <= k < row:
                    perm.append((g * row + j, (partner[g][1] if cross else g) * row + k))
        return lax.ppermute(value, ("gx", "row"), perm)

    def call(kernel, name, outs, ins, extra=(), **more):
        return pl.pallas_call(
            kernel, name=name, out_shape=outs, in_specs=[VM] * len(ins), out_specs=[VM] * len(outs),
            scratch_shapes=list(scratch) + list(extra), compiler_params=PARAMS, **more,
        )(*ins)

    hbm = lambda a: pltpu.with_memory_space_constraint(a, pltpu.HBM)
    small = lambda kernel, name, outs, *ins, extra=(): pl.pallas_call(
        kernel, name=name, out_shape=outs, in_specs=[VM] * len(ins),
        out_specs=[VM] * len(outs) if isinstance(outs, list) else VM, scratch_shapes=extra, compiler_params=PARAMS)(*ins)
    duo = pltpu.VMEM(pair.shape, f32)
    n, e = 20 * rows, 20 * cells
    own, other, outer, base_own, base_send, rest, table = pl.pallas_call(
        load_kernel, name="load",
        out_shape=[block, block, shape(26, rows, width), base, base, shape(34, rows, width),
                   jax.ShapeDtypeStruct(tab.shape, tab.dtype)],
        in_specs=[HB] * 5, out_specs=[VM] * 7, scratch_shapes=[pltpu.SemaphoreType.DMA((37,))],
        compiler_params=PARAMS,
    )(hbm(halves(adjoint_vectors)), hbm(halves(base_density)), hbm(halves(base_velocity)),
      hbm(halves(base_pressure)), hbm(tab))
    outer, rest = trade(outer), trade(rest)
    part_own, xp_own, xd_own, rp_own, first, rp_other, second = call(
        own_first_kernel, "own_1", [block, pair, pair, edge, edge, edge, edge],
        (own, other, base_own, base_send, table), (pltpu.VMEM(edge.shape, f32), pltpu.VMEM(edge.shape, f32)))
    message, rd_own_in = small(
        pack_kernel, "pack", [shape(2 * e, width), edge], rp_own, *swap_both(row_swaps, "row", first, second))
    faces = swap_both(z_swaps, "gx", *small(face_kernel, "face", [pair, pair], outer, xd_own, message))
    message = trade(message)
    w_par, base_par, part_par, xp_par = call(
        partner_first_kernel, "partner_1", [block, base, block, pair], (outer, rest, table))
    faces2 = swap_both(z_swaps, "gx", *small(
        outer_faces_kernel, "outer_faces", [pair, pair], part_own, part_par, *faces, rp_other, rd_own_in, message,
        base_own, base_par, extra=[duo, duo]))
    inner, outer, xp_par2, rd_par = call(
        partner_second_kernel, "partner_2", [shape(n + e, width), pair, pair, edge],
        (w_par, part_par, xp_own, *faces, message, part_own, xp_par, rp_other, rd_own_in, base_own, base_par, table),
        (whole, whole, duo, duo))
    inner = trade(inner)
    part_own, rp_own, rd_own = call(
        own_second_kernel, "own_2", [block, edge, edge],
        (own, part_own, xp_par, *faces, rp_other, rd_own_in, base_own, table, rd_par), (whole,))
    outer = small(finish_kernel, "finish", pair, outer, *faces2, rd_own)
    outer = trade(outer)
    rd_other_in = beside(rd_par, True, 0)
    rd_own_in = beside(rd_own, False, 0)
    xp_par = xp_par2
    full = shape(2, 5, cells, 2, rows, width)
    last = dict(out_shape=full, out_specs=HB, compiler_params=PARAMS)
    out = pl.pallas_call(own_last_kernel, name="own_3", in_specs=[VM] * 6, scratch_shapes=[whole, pltpu.SemaphoreType.DMA], **last)(
        part_own, xp_par, *faces2, inner, rd_own_in)
    out = pl.pallas_call(
        other_last_kernel, name="other_3", in_specs=[VM] * 4 + [HB], input_output_aliases={4: 0},
        scratch_shapes=[whole, pltpu.SemaphoreType.DMA((2,))], **last,
    )(inner, outer, rp_own, rd_other_in, out)
    return out.reshape(adjoint_vectors.shape)


def solution(mesh):
    in_specs = (
        P(None, None, "gx", "row", None),
        P("gx", "row", None),
        P(None, "gx", "row", None),
        P("gx", "row", None),
    )
    out_specs = P(None, None, "gx", "row", None)
    return jax.shard_map(local, mesh=mesh, in_specs=in_specs, out_specs=out_specs, check_vma=False)
```
